32 devices in a mesh: shift: 2 (over y), space: 4 (over z), orb: 2 (over x), grid: 2 (over core).
Axes of the slice: x: 2, y: 2, z: 4, core: 2. Of those that a mesh axis runs over, the one named last changes fastest.
Arguments:
- support: bfloat16 [128, 9, 15, 256], P(('shift', 'space', 'orb'), None, None, 'grid'), parts along dimension 0, may hold values from -0.75 to 0.75
- anchor: int32 [128], P(('shift', 'space', 'orb')), parts along dimension 0, may hold values from 0 to 63, as said below
- kernel: float32 [512, 9, 9], P(('shift', 'space', 'orb')), parts along dimension 0, may hold values from -2.1 to 2.1
- pair_owner: int32 [512], P(('shift', 'space', 'orb')), parts along dimension 0, may hold values from 0 to 63, as said below
- pair_partner: int32 [512], P(('shift', 'space', 'orb')), parts along dimension 0, may hold values from 0 to 63, as said below
- pair_live: int32 [512], P(('shift', 'space', 'orb')), parts along dimension 0, may hold values 0 or 1
- v_ext: float32 [128, 256], P(('shift', 'space'), 'grid'), parts along dimension 0, may hold values from -6 to 6
Outputs:
- density: float32 [128, 256], P(('shift', 'space'), 'grid'), parts along dimension 0
- hamiltonian: float32 [512, 9, 9], P(('shift', 'space', 'orb')), parts along dimension 0
The draws below stay inside these ranges and needn't reach their ends.
There are 2 independent parts, one for each index of `shift`. The reference program is written for one: setup_inputs(seed, part) draws one part's arguments, and reference() takes and returns one part's arrays. A program takes and returns all parts, laid end to end along the dimension named above; each array names one. Nothing has to cross between parts.
Inputs may be any that keep to these rules, and one draw needn't show every extreme that they name: Atom a lies in spatial domain a // 16, and its box starts at a plane of that domain: anchor[a] // 16 = a // 16. The owner of slot p is one of the 8 atoms of block p // 32: pair_owner[p] // 8 = p // 32. `pair_partner`: the partner of a slot lies in its owner's spatial domain or in one of the two adjacent domains, counted periodically, and its box shares at least one plane with the owner's box: |gap| <= 14.
All inputs are finite; a program needn't handle non-finite values. No bound on the sum of `pair_live` on one device may be relied on, other than what follows from the above.
Results may differ from the reference program's by a relative error of at most 0.0028.
Values may be sent and summed in bfloat16 or wider, within the bound.
No kernel may reach another device: no remote copies, remote signals or barrier semaphores. Data moves between devices by JAX's collectives and lax.ppermute only.
A program may use at most 64 MiB of HBM per device.

```python
import jax
import jax.numpy as jnp
from jax import lax

NSF = 9
BZ = 15
PLANE = 256
SLAB = 16
ATOM_DEV = 8
PAIR_DEV = 32
ATOM_DOM = 16
ATOMS = 64
PAIRS = 256
NZ = 64


def anchor_table(key):
    rows = jnp.arange(ATOMS, dtype=jnp.int32)
    home = rows // ATOM_DOM
    offset = jax.random.randint(jax.random.fold_in(key, 11), (ATOMS,), 0, SLAB, dtype=jnp.int32)
    return (home * SLAB + offset).astype(jnp.int32)


def owner_table(key):
    slots = jnp.arange(PAIRS, dtype=jnp.int32)
    block = slots // PAIR_DEV
    pick = jax.random.randint(jax.random.fold_in(key, 23), (PAIRS,), 0, ATOM_DEV, dtype=jnp.int32)
    return (block * ATOM_DEV + pick).astype(jnp.int32)


def draw_anchor(key, part):
    return anchor_table(key)


def draw_pair_owner(key, part):
    return owner_table(key)


def draw_pair_partner(key, part):
    starts = anchor_table(key)
    owners = owner_table(key)
    domains = ATOMS // ATOM_DOM
    home = owners // ATOM_DOM
    width = 3 * ATOM_DOM
    column = jnp.arange(width, dtype=jnp.int32)[None, :]
    cand_domain = (home[:, None] - 1 + column // ATOM_DOM + domains) % domains
    candidate = (cand_domain * ATOM_DOM + column % ATOM_DOM).astype(jnp.int32)
    gap = (starts[owners][:, None] - starts[candidate] + NZ // 2) % NZ - NZ // 2
    fits = jnp.abs(gap) <= BZ - 1
    noise = jax.random.randint(jax.random.fold_in(key, 37), (PAIRS, width), 0, 1048576, dtype=jnp.int32)
    score = jnp.where(fits, noise * width + column, -1)
    best = jnp.argmax(score, axis=1).astype(jnp.int32)
    return jnp.take_along_axis(candidate, best[:, None], axis=1)[:, 0].astype(jnp.int32)


def touch_ends(result, key, low, high):
    shape = result.shape
    place = [jax.random.randint(jax.random.fold_in(key, axis), (), 0, shape[axis]) for axis in range(len(shape))]
    result = result.at[tuple(place)].set(low)
    longest = shape.index(max(shape))
    place[longest] = (place[longest] + 1) % shape[longest]
    return result.at[tuple(place)].set(high)


def steps_of(key, shape, pieces, low, high):
    gain = 1.0
    for position, shards_of in pieces:
        steps = jax.random.uniform(jax.random.fold_in(jax.random.fold_in(key, 6), position), (shards_of,), jnp.float32, low / len(pieces), high / len(pieces))
        gain = gain * jnp.repeat(jnp.exp(steps), shape[position] // shards_of).reshape((-1,) + (1,) * (len(shape) - 1 - position))
    return gain


def scatter_about(stream_key, shape, scale, limit, split=(), kind=jnp.bfloat16):
    level = steps_of(stream_key, shape, split, -0.22, 0.18) if split else 1.0
    result = jax.random.normal(stream_key, shape, jnp.float32) * scale * level
    return jnp.minimum(jnp.maximum(result, -limit), limit).astype(kind)


def setup_inputs(seed: int = 0, part: int = 0) -> dict:
    keys = jax.random.split(jax.random.key(seed), 8)
    part_splits = jax.random.split(jax.random.fold_in(keys[7], part), 8)
    return {
        "support": scatter_about(part_splits[0], (ATOMS, NSF, BZ, PLANE), 0.125, 0.75, ((0, 8), (3, 2))),
        "anchor": draw_anchor(jax.random.fold_in(jax.random.fold_in(keys[7], part), 71), part),
        "kernel": scatter_about(part_splits[2], (PAIRS, NSF, NSF), 0.35, 2.1, ((0, 8),), jnp.float32),
        "pair_owner": draw_pair_owner(jax.random.fold_in(jax.random.fold_in(keys[7], part), 71), part),
        "pair_partner": draw_pair_partner(jax.random.fold_in(jax.random.fold_in(keys[7], part), 71), part),
        "pair_live": touch_ends((jax.random.randint(part_splits[5], (PAIRS,), 0, 4) < 3).astype(jnp.int32), jax.random.fold_in(part_splits[5], 1), 0, 1),
        "v_ext": scatter_about(part_splits[6], (NZ, PLANE), 1.0, 6.0, ((0, 4), (1, 2)), jnp.float32),
    }


def shift_planes(rows, plane_gap, box_depth):
    index = jnp.arange(box_depth, dtype=jnp.int32)[None, :] + plane_gap[:, None]
    inside = (index >= 0) & (index < box_depth)
    picked = jnp.take_along_axis(rows, jnp.clip(index, 0, box_depth - 1)[:, None, :, None], axis=2)
    return jnp.where(inside[:, None, :, None], picked, jnp.zeros_like(picked))

def reference(support, anchor, kernel, pair_owner, pair_partner, pair_live, v_ext):
    blocks = PAIRS // PAIR_DEV
    owners = pair_owner.reshape(blocks, PAIR_DEV)
    partners = pair_partner.reshape(blocks, PAIR_DEV)
    live = pair_live.astype(jnp.float32).reshape(blocks, PAIR_DEV)
    weights = kernel.reshape(blocks, PAIR_DEV, NSF, NSF)
    block_ids = jnp.arange(blocks, dtype=jnp.int32)

    def moved_rows(own, part):
        plane_gap = (anchor[own] - anchor[part] + NZ // 2) % NZ - NZ // 2
        return shift_planes(support[part], plane_gap.astype(jnp.int32), BZ)

    def block_aux(items):
        own, part, alive, kern, block = items
        moved = moved_rows(own, part).astype(jnp.float32)
        terms = jnp.einsum('pst,ptjq->psjq', kern * alive[:, None, None], moved, precision=lax.Precision.HIGHEST)
        local = (own - block * ATOM_DEV).astype(jnp.int32)
        return jax.ops.segment_sum(terms, local, num_segments=ATOM_DEV)
    aux = lax.map(block_aux, (owners, partners, live, weights, block_ids))
    aux = aux.reshape(ATOMS, NSF, BZ, PLANE)
    deposit = lax.optimization_barrier(jnp.sum(support.astype(jnp.float32) * aux, axis=1))
    planes = (anchor[:, None] + jnp.arange(BZ, dtype=jnp.int32)[None, :]) % NZ
    density = jnp.zeros((NZ, PLANE), jnp.float32).at[planes.reshape(-1)].add(deposit.reshape(-1, PLANE))
    potential = v_ext + density / jnp.sqrt(1.0 + density * density)
    box_potential = potential[planes]
    weighted = (support.astype(jnp.float32) * box_potential[:, None, :, :]).astype(jnp.bfloat16)

    def block_ham(items):
        own, part, alive = items
        moved = moved_rows(own, part).astype(jnp.float32)
        rows = weighted[own].astype(jnp.float32)
        blocks_out = jnp.einsum('psjq,ptjq->pst', rows, moved, precision=lax.Precision.HIGHEST)
        return blocks_out * alive[:, None, None]
    hamiltonian = lax.map(block_ham, (owners, partners, live)).reshape(PAIRS, NSF, NSF)
    return (density, hamiltonian)
```

```python
import functools

import jax
import jax.numpy as jnp
from jax import lax
from jax.experimental import pallas as pl
from jax.experimental.pallas import tpu as pltpu
from jax.sharding import PartitionSpec as P

LANES = 128
F32 = jnp.float32
BF16 = jnp.bfloat16


def moved_by(value, axes, steps):
    sizes = [lax.axis_size(axis) for axis in axes]
    pairs = []
    total = 1
    for size in sizes:
        total *= size
    for source in range(total):
        rest, place = source, []
        for size in reversed(sizes):
            place.insert(0, rest % size)
            rest //= size
        target = 0
        for size, here, step in zip(sizes, place, steps):
            target = target * size + (here + step) % size
        pairs.append((source, target))
    return lax.ppermute(value, axes if len(axes) > 1 else axes[0], pairs)


def round_up(count, unit):
    return (count + unit - 1) // unit * unit


def pack_kernel(dims, orb_ref, anchor_ref, x_ref, k_ref, owner_ref, live_ref, code_ref, *rest):
    atoms, functions, depth, points, slab, ways, reach, pairs = dims
    own_refs, next_refs = rest[:ways], rest[ways : 2 * ways]
    pair_ref, k_pad, row_pad = rest[2 * ways :]
    planes = slab // ways
    boxes = -(-depth // ways)
    orb = orb_ref[0]
    atom = lax.broadcasted_iota(jnp.int32, (atoms, points), 0)
    offset = jnp.zeros((atoms, points), jnp.int32)
    for a in range(atoms):
        offset = jnp.where(atom == a, lax.rem(anchor_ref[a], slab), offset)
    zero = jnp.zeros((atoms, points), F32)
    masks = []
    for k in range(ways):
        residue = lax.rem(orb + k, ways)
        start = offset - residue
        shift = jnp.zeros((atoms, points), jnp.int32)
        for low in range(slab // ways):
            shift = shift + (start > low * ways).astype(jnp.int32)
        phase = shift * ways - start
        bits, size = [], 1
        while size <= -(-(slab - 1) // ways):
            bits.append((size, (shift & size) != 0))
            size *= 2
        masks.append(([phase == e for e in range(ways)], bits))
    for s in range(functions):
        tiles = [x_ref[s, j].astype(F32) for j in range(depth)]
        for k in range(ways):
            phases, bits = masks[k]
            line = []
            for m in range(boxes):
                pick = zero
                for e in range(ways):
                    j = m * ways + e
                    pick = jnp.where(phases[e], tiles[j] if j < depth else zero, pick)
                line.append(pick)
            for size, mask in bits:
                length = min(len(line) + size, planes + reach)
                line = [
                    jnp.where(
                        mask,
                        line[h - size] if h >= size else zero,
                        line[h] if h < len(line) else zero,
                    )
                    for h in range(length)
                ]
            line = line + [zero] * (planes + reach - len(line))
            rows = pl.ds(s * atoms, atoms)
            for h in range(planes):
                own_refs[k][h, rows, :] = line[h].astype(BF16)
            for h in range(reach):
                next_refs[k][h, rows, :] = line[planes + h].astype(BF16)
    per = LANES // pairs
    groups = -(-functions // per)
    k_pad[...] = jnp.zeros_like(k_pad)
    k_pad[:, :functions, :pairs] = k_ref[...]
    pair_ref[...] = jnp.zeros_like(pair_ref)
    for s in range(functions):
        for g in range(groups):
            row = jnp.zeros((1, LANES), F32)
            for i in range(per):
                t = g * per + i
                if t < functions:
                    piece = k_pad[s, t : t + 1, :]
                    row = row + (pltpu.roll(piece, i * pairs, 1) if i else piece)
            pair_ref[s : s + 1, g * LANES : (g + 1) * LANES] = row
    row_pad[...] = jnp.zeros_like(row_pad)
    row_pad[0:1, :pairs] = owner_ref[...].astype(F32)
    row_pad[1:2, :pairs] = live_ref[...].astype(F32)
    row_pad[2:3, :pairs] = code_ref[...].astype(F32)
    index = row_pad[...]
    wide = index
    for i in range(1, per):
        wide = wide + pltpu.roll(index, i * pairs, 1)
    for g in range(groups):
        pair_ref[functions : functions + 3, g * LANES : (g + 1) * LANES] = wide[0:3]


def main_kernel(dims, orb_ref, v_ref, *rest):
    atoms, functions, depth, points, slab, ways, reach, pairs = dims
    planes = slab // ways
    sources = 2 * ways
    source_refs = rest[:sources]
    pair_refs = rest[sources : 2 * sources]
    own_out, low_out, f_ref, w_ref, d_ref, rt_ref, own_ref, h_ref = rest[2 * sources :]
    block = functions * atoms
    rows = sources * block
    padded = f_ref.shape[0]
    lanes = pair_refs[0].shape[1]
    orb = orb_ref[0]
    per_domain = atoms * ways
    for c in range(sources):
        count = source_refs[c].shape[0]
        for h in range(planes):
            place = (pl.ds(c * block, block), pl.ds(h * points, points))
            if h < count:
                f_ref[place] = source_refs[c][h]
            else:
                f_ref[place] = jnp.zeros((block, points), BF16)
    if padded > rows:
        f_ref[rows:, :] = jnp.zeros((padded - rows, planes * points), BF16)
    row_id = lax.broadcasted_iota(jnp.int32, (padded, lanes), 0)
    atom_id = lax.broadcasted_iota(jnp.int32, (atoms, lanes), 0)
    lane_id = lax.broadcasted_iota(jnp.int32, (1, lanes), 1)
    function_id = jnp.zeros((1, lanes), jnp.int32)
    for t in range(1, lanes // pairs):
        function_id = function_id + (lane_id >= t * pairs).astype(jnp.int32)
    for c in range(sources):
        info = pair_refs[c]
        owner = info[functions : functions + 1, :].astype(jnp.int32)
        live = info[functions + 1 : functions + 2, :]
        code = info[functions + 2 : functions + 3, :].astype(jnp.int32)
        domain = (code >= per_domain).astype(jnp.int32) + (code >= 2 * per_domain).astype(jnp.int32)
        inside = code - domain * per_domain
        orb_of = jnp.zeros((1, lanes), jnp.int32)
        for i in range(1, ways):
            orb_of = orb_of + (inside >= i * atoms).astype(jnp.int32)
        local = inside - orb_of * atoms
        slot = orb - orb_of
        slot = jnp.where(slot < 0, slot + ways, slot)
        if c < ways:
            slot = slot + jnp.where(domain == 0, ways, 0)
            valid = domain <= 1
        else:
            slot = slot + jnp.where(domain == 1, ways, 0)
            valid = domain >= 1
        valid = valid & (lane_id < functions * pairs)
        target = jnp.where(valid, slot * block + function_id * atoms + local, -1)
        table = jnp.where(row_id == target, 1.0, 0.0).astype(BF16)
        rt_ref[c] = table
        own = jnp.where(atom_id == owner, live, 0.0)
        own_ref[c] = own
        left = jnp.concatenate([info[s : s + 1, :] * own for s in range(functions)], axis=0)
        high = left.astype(BF16)
        low = (left - high.astype(F32)).astype(BF16)
        contract = (((1,), (1,)), ((), ()))
        part = lax.dot_general(high, table, contract, preferred_element_type=F32)
        part = part + lax.dot_general(low, table, contract, preferred_element_type=F32)
        high = part.astype(BF16)
        low = (part - high.astype(F32)).astype(BF16)
        d_ref[c * block : (c + 1) * block, :padded] = high
        d_ref[c * block : (c + 1) * block, padded:] = low
    f_all = f_ref[...]
    doubled = jnp.concatenate([f_all, f_all], axis=0)
    aux = jnp.dot(d_ref[...], doubled, preferred_element_type=F32)
    density = jnp.sum(aux * f_ref[:rows, :].astype(F32), axis=0, keepdims=True)
    v_ext = jnp.concatenate([v_ref[pl.ds(h * ways + orb, 1), :] for h in range(planes)], axis=1)
    potential = v_ext + density / jnp.sqrt(1.0 + density * density)
    w_ref[...] = (f_ref[:rows, :].astype(F32) * potential).astype(BF16)
    blocks = lax.dot_general(
        w_ref[...], f_all, (((1,), (1,)), ((), ())), preferred_element_type=F32
    )
    h_ref[...] = blocks
    own_out[...] = jnp.zeros_like(own_out)
    low_out[...] = jnp.zeros_like(low_out)
    for c in range(sources):
        part = h_ref[c * block : (c + 1) * block, :]
        high = part.astype(BF16)
        low = (part - high.astype(F32)).astype(BF16)
        table = rt_ref[c]
        spread = jnp.dot(high, table, preferred_element_type=F32)
        spread = spread + jnp.dot(low, table, preferred_element_type=F32)
        own = own_ref[c]
        picked = jnp.concatenate(
            [
                jnp.sum(spread[s * atoms : (s + 1) * atoms] * own, axis=0, keepdims=True)
                for s in range(functions)
            ],
            axis=0,
        )
        if c < ways:
            own_out[c, :functions, :] = picked
            for h in range(planes):
                own_out[c, 16 + h : 17 + h, :points] = density[:, h * points : (h + 1) * points]
        else:
            low_out[c - ways, :functions, :] = picked


def final_kernel(dims, orb_ref, mine_ref, other_ref, *rest):
    atoms, functions, depth, points, slab, ways, reach, pairs = dims
    planes = slab // ways
    message_refs = rest[:ways]
    density_ref, out_ref, pad_ref = rest[ways:]
    orb = orb_ref[0]
    for k in range(ways):
        residue = lax.rem(orb + k, ways)
        for h in range(planes):
            density_ref[pl.ds(h * ways + residue, 1), :] = message_refs[k][16 + h : 17 + h, :points]
    total = mine_ref[...] + other_ref[...]
    per = LANES // pairs
    for t in range(functions):
        g, i = t // per, t % per
        piece = total[:, g * LANES : (g + 1) * LANES]
        if i:
            piece = pltpu.roll(piece, LANES - i * pairs, 1)
        pad_ref[...] = piece
        for s in range(functions):
            out_ref[s, t : t + 1, :] = pad_ref[s : s + 1, :pairs]


def on_device(support, anchor, kernel, pair_owner, pair_partner, pair_live, v_ext):
    atoms, functions, depth, points = support.shape
    pairs = kernel.shape[0]
    slab = v_ext.shape[0]
    ways = lax.axis_size("orb")
    space = lax.axis_size("space")
    per_domain = atoms * ways
    planes = slab // ways
    reach = min((depth - 2) // ways + 1, planes)
    dims = (atoms, functions, depth, points, slab, ways, reach, pairs)
    domain = lax.axis_index("space")
    orb = lax.axis_index("orb")
    orb_row = jnp.reshape(orb, (1,)).astype(jnp.int32)
    block = functions * atoms
    lanes = round_up(functions * pairs, LANES)
    smem = pl.BlockSpec(memory_space=pltpu.SMEM)
    vmem = pl.BlockSpec(memory_space=pltpu.VMEM)

    relative = (pair_partner // per_domain - domain + 1 + space) % space
    code = (relative * per_domain + pair_partner % per_domain).reshape(1, pairs)
    owner = (pair_owner % atoms).reshape(1, pairs)
    live = pair_live.reshape(1, pairs)

    packed = pl.pallas_call(
        functools.partial(pack_kernel, dims),
        out_shape=[jax.ShapeDtypeStruct((planes, block, points), BF16)] * ways
        + [jax.ShapeDtypeStruct((reach, block, points), BF16)] * ways
        + [jax.ShapeDtypeStruct((16, lanes), F32)],
        in_specs=[smem, smem] + [vmem] * 5,
        out_specs=[vmem] * (2 * ways + 1),
        scratch_shapes=[pltpu.VMEM((functions, 16, LANES), F32), pltpu.VMEM((8, LANES), F32)],
        name="pack",
    )(
        orb_row,
        anchor,
        support.transpose(1, 2, 0, 3),
        kernel.transpose(1, 2, 0),
        owner,
        live,
        code,
    )
    own, onward, pair_rows = packed[:ways], packed[ways : 2 * ways], packed[2 * ways]
    sources, pair_sources = [own[0]], [pair_rows]
    for k in range(1, ways):
        sources.append(moved_by(own[k], ("orb",), (k,)))
        pair_sources.append(moved_by(pair_rows, ("orb",), (k,)))
    for k in range(ways):
        sources.append(moved_by(onward[k], ("space", "orb"), (1, k)))
        pair_sources.append(moved_by(pair_rows, ("space", "orb"), (1, k)))

    rows = 2 * ways * block
    padded = round_up(rows, LANES)
    own_part, low_part = pl.pallas_call(
        functools.partial(main_kernel, dims),
        out_shape=[
            jax.ShapeDtypeStruct((ways, 16 + round_up(planes, 8), lanes), F32),
            jax.ShapeDtypeStruct((ways, 16, lanes), F32),
        ],
        in_specs=[smem] + [vmem] * (1 + 4 * ways),
        out_specs=[vmem] * 2,
        scratch_shapes=[
            pltpu.VMEM((padded, planes * points), BF16),
            pltpu.VMEM((rows, planes * points), BF16),
            pltpu.VMEM((rows, 2 * padded), BF16),
            pltpu.VMEM((2 * ways, padded, lanes), BF16),
            pltpu.VMEM((2 * ways, atoms, lanes), F32),
            pltpu.VMEM((rows, padded), F32),
        ],
        name="main",
    )(orb_row, v_ext, *sources, *pair_sources)

    from_above = moved_by(low_part, ("space",), (-1,))
    total = own_part + jnp.pad(from_above, ((0, 0), (0, own_part.shape[1] - 16), (0, 0)))
    messages = [total[0]]
    mine = total[0, :16]
    for k in range(1, ways):
        message = moved_by(total[k], ("orb",), (-k,))
        messages.append(message)
        mine = mine + message[:16]
    other = mine
    shares = lax.axis_size("grid")
    other = moved_by(mine, ("grid",), (1,))
    for k in range(2, shares):
        other = other + moved_by(mine, ("grid",), (k,))
    density, blocks = pl.pallas_call(
        functools.partial(final_kernel, dims),
        out_shape=[
            jax.ShapeDtypeStruct((slab, points), F32),
            jax.ShapeDtypeStruct((functions, functions, pairs), F32),
        ],
        in_specs=[smem] + [vmem] * (2 + ways),
        out_specs=[vmem] * 2,
        scratch_shapes=[pltpu.VMEM((16, LANES), F32)],
        name="final",
    )(orb_row, mine, other, *messages)
    return (density, blocks.transpose(2, 0, 1))


def solution(mesh):
    placed = (
        P(("shift", "space", "orb"), None, None, "grid"),
        P(("shift", "space", "orb")),
        P(("shift", "space", "orb"), None, None),
        P(("shift", "space", "orb")),
        P(("shift", "space", "orb")),
        P(("shift", "space", "orb")),
        P(("shift", "space"), "grid"),
    )
    return jax.shard_map(
        on_device,
        mesh=mesh,
        in_specs=placed,
        out_specs=(P(("shift", "space"), "grid"), P(("shift", "space", "orb"), None, None)),
        check_vma=False,
    )
```

```python
import functools

import jax
import jax.numpy as jnp
from jax import lax
from jax.experimental import pallas as pl
from jax.experimental.pallas import tpu as pltpu
from jax.sharding import PartitionSpec as P


LANES = 128
F32 = jnp.float32
BF16 = jnp.bfloat16


def moved_by(value, axes, steps):
    sizes = [lax.axis_size(axis) for axis in axes]
    pairs = []
    total = 1
    for size in sizes:
        total *= size
    for source in range(total):
        rest, place = source, []
        for size in reversed(sizes):
            place.insert(0, rest % size)
            rest //= size
        target = 0
        for size, here, step in zip(sizes, place, steps):
            target = target * size + (here + step) % size
        pairs.append((source, target))
    return lax.ppermute(value, axes if len(axes) > 1 else axes[0], pairs)


def round_up(count, unit):
    return (count + unit - 1) // unit * unit


def fixed(value):
    return pltpu.with_memory_space_constraint(value, pltpu.HBM)


def pack_kernel(dims, orb_ref, domain_ref, *rest):
    atoms, functions, depth, points, slab, ways, reach, pairs, space = dims
    given, rest = rest[:6], rest[6:]
    own_refs, next_refs = rest[:ways], rest[ways : 2 * ways]
    k_pad, row_pad, *held, x_sem, sems = rest[2 * ways :]
    anchor_ref, x_ref, k_ref, owner_ref, partner_ref, live_ref = held
    copies = [
        pltpu.make_async_copy(given[i], held[i], sems.at[i]) for i in range(6) if i != 1
    ]
    x_copies = [
        pltpu.make_async_copy(given[1].at[s], x_ref.at[s], x_sem.at[s]) for s in range(functions)
    ]
    copies[0].start()
    for copy in x_copies:
        copy.start()
    for copy in copies[1:]:
        copy.start()
    copies[0].wait()
    planes = slab // ways
    boxes = -(-depth // ways)
    orb, domain = orb_ref[0], domain_ref[0]
    atom = lax.broadcasted_iota(jnp.int32, (atoms, points), 0)
    offset = jnp.zeros((atoms, points), jnp.int32)
    for a in range(atoms):
        offset = jnp.where(atom == a, lax.rem(anchor_ref[a], slab), offset)
    zero = jnp.zeros((atoms, points), F32)
    masks = []
    for k in range(ways):
        residue = lax.rem(orb + k, ways)
        start = offset - residue
        shift = jnp.zeros((atoms, points), jnp.int32)
        for low in range(slab // ways):
            shift = shift + (start > low * ways).astype(jnp.int32)
        phase = shift * ways - start
        bits, size = [], 1
        while size <= -(-(slab - 1) // ways):
            bits.append((size, (shift & size) != 0))
            size *= 2
        masks.append(([phase == e for e in range(ways)], bits))
    for s in range(functions):
        x_copies[s].wait()
        tiles = [x_ref[s, j].astype(F32) for j in range(depth)]
        for k in range(ways):
            phases, bits = masks[k]
            line = []
            for m in range(boxes):
                pick = zero
                for e in range(ways):
                    j = m * ways + e
                    pick = jnp.where(phases[e], tiles[j] if j < depth else zero, pick)
                line.append(pick)
            for size, mask in bits:
                length = min(len(line) + size, planes + reach)
                line = [
                    jnp.where(
                        mask,
                        line[h - size] if h >= size else zero,
                        line[h] if h < len(line) else zero,
                    )
                    for h in range(length)
                ]
            line = line + [zero] * (planes + reach - len(line))
            rows = pl.ds(s * atoms, atoms)
            for h in range(planes):
                own_refs[k][h, rows, :] = line[h].astype(BF16)
            for h in range(reach):
                next_refs[k][h, rows, :] = line[planes + h].astype(BF16)
    per = LANES // pairs
    groups = -(-functions // per)
    for copy in copies[1:]:
        copy.wait()
    k_pad[...] = jnp.zeros_like(k_pad)
    k_pad[:, :functions, :pairs] = k_ref[...]
    row_pad[...] = jnp.zeros_like(row_pad)
    for s in range(functions):
        for g in range(groups):
            row = jnp.zeros((1, LANES), F32)
            for i in range(per):
                t = g * per + i
                if t < functions:
                    piece = k_pad[s, t : t + 1, :]
                    row = row + (pltpu.roll(piece, i * pairs, 1) if i else piece)
            row_pad[g * functions + s : g * functions + s + 1, :] = row
    per_domain = atoms * ways
    owner = owner_ref[...] - (domain * ways + orb) * atoms
    partner = partner_ref[...]
    home = jnp.floor((partner.astype(F32) + 0.5) * (1.0 / per_domain)).astype(jnp.int32)
    relative = home - domain + 1
    relative = jnp.where(relative < 0, relative + space, relative)
    relative = jnp.where(relative >= space, relative - space, relative)
    code = relative * per_domain + partner - home * per_domain
    base = groups * functions
    row_pad[base : base + 1, :pairs] = owner.astype(F32)
    row_pad[base + 1 : base + 2, :pairs] = live_ref[...].astype(F32)
    row_pad[base + 2 : base + 3, :pairs] = code.astype(F32)
    index = row_pad[base : base + 3, :]
    wide = index
    for i in range(1, per):
        wide = wide + pltpu.roll(index, i * pairs, 1)
    row_pad[base : base + 3, :] = wide
    info = row_pad[...]
    high = info.astype(BF16)
    low = (info - high.astype(F32)).astype(BF16)
    height = info.shape[0]
    for refs, last in ((own_refs, planes), (next_refs, reach)):
        for k in range(ways):
            refs[k][last, 0:height, :] = high
            refs[k][last, height : 2 * height, :] = low


def main_kernel(dims, orb_ref, v_ref, *rest):
    atoms, functions, _, points, slab, ways, _, pairs, _ = dims
    planes = slab // ways
    sources = 2 * ways
    source_refs = rest[:sources]
    own_out, low_out, f_ref, w_ref, d_ref, table_ref, own_ref, info_ref = rest[sources:]
    block = functions * atoms
    band = sources * atoms
    rows = functions * band
    padded = f_ref.shape[0]
    per = LANES // pairs
    groups = -(-functions // per)
    height = info_ref.shape[0] // 2
    spans, first = [], 0
    most = table_ref.shape[1] // band
    while first < functions:
        count = min(most, functions - first)
        spans.append((first, count, round_up(count * pairs, LANES)))
        first += count
    orb = orb_ref[0]
    per_domain = atoms * ways
    contract = (((1,), (1,)), ((), ()))
    for h in range(planes):
        for c in range(sources):
            last = source_refs[c].shape[0] - 1
            for s in range(functions):
                place = (pl.ds((s * sources + c) * atoms, atoms), pl.ds(h * points, points))
                if h < last:
                    f_ref[place] = source_refs[c][h, s * atoms : (s + 1) * atoms, :]
                else:
                    f_ref[place] = jnp.zeros((atoms, points), BF16)
    if padded > rows:
        f_ref[rows:, :] = jnp.zeros((padded - rows, planes * points), BF16)
    tail = rows // LANES * LANES
    if padded > tail:
        d_ref[:, tail:padded] = jnp.zeros((rows, padded - tail), BF16)
        d_ref[:, padded + tail :] = jnp.zeros((rows, padded - tail), BF16)
    size = table_ref.shape[1:]
    row_id = lax.broadcasted_iota(jnp.int32, size, 0)
    lane_id = lax.broadcasted_iota(jnp.int32, (1, size[1]), 1)
    function_id = jnp.zeros((1, size[1]), jnp.int32)
    for t in range(1, size[1] // pairs):
        function_id = function_id + (lane_id >= t * pairs).astype(jnp.int32)
    atom_id = lax.broadcasted_iota(jnp.int32, (atoms, LANES), 0)
    base = groups * functions
    for c in range(sources):
        last = source_refs[c].shape[0] - 1
        pair_high = source_refs[c][last, 0:height, :].astype(F32)
        pair_low = source_refs[c][last, height : 2 * height, :].astype(F32)
        owner = pair_high[base : base + 1, :].astype(jnp.int32)
        live = pair_high[base + 1 : base + 2, :]
        code = pair_high[base + 2 : base + 3, :].astype(jnp.int32)
        domain = (code >= per_domain).astype(jnp.int32) + (code >= 2 * per_domain).astype(jnp.int32)
        inside = code - domain * per_domain
        orb_of = jnp.zeros(code.shape, jnp.int32)
        for i in range(1, ways):
            orb_of = orb_of + (inside >= i * atoms).astype(jnp.int32)
        local = inside - orb_of * atoms
        slot = orb - orb_of
        slot = jnp.where(slot < 0, slot + ways, slot)
        if c < ways:
            slot = slot + jnp.where(domain == 0, ways, 0)
            valid = domain <= 1
        else:
            slot = slot + jnp.where(domain == 1, ways, 0)
            valid = domain >= 1
        inner = jnp.where(valid, slot * atoms + local, -padded * LANES)
        inner = jnp.concatenate([inner] * (size[1] // LANES), axis=1)
        target = inner + function_id * band
        table = jnp.where(row_id == target, 1.0, 0.0).astype(BF16)
        table_ref[c] = table
        own = jnp.where(atom_id == owner, live, 0.0)
        own_ref[c] = own
        for first, count, lanes in spans:
            parts = []
            for pair_rows in (pair_high, pair_low):
                for s in range(functions):
                    parts.append(
                        jnp.concatenate(
                            [
                                pair_rows[g * functions + s : g * functions + s + 1, :] * own
                                for g in range(first // per, first // per + lanes // LANES)
                            ],
                            axis=1,
                        )
                    )
            left = jnp.concatenate(parts, axis=0).astype(BF16)
            cols = count * band
            part = lax.dot_general(
                left, table_ref[c, :cols, :lanes], contract, preferred_element_type=F32
            )
            part = part[:block] + part[block:]
            high = part.astype(BF16)
            low = (part - high.astype(F32)).astype(BF16)
            for s in range(functions):
                place = pl.ds((s * sources + c) * atoms, atoms)
                d_ref[place, first * band : first * band + cols] = high[s * atoms : (s + 1) * atoms]
                d_ref[place, padded + first * band : padded + first * band + cols] = low[
                    s * atoms : (s + 1) * atoms
                ]
    f_all = f_ref[...]
    aux = jnp.dot(d_ref[...], jnp.concatenate([f_all, f_all], axis=0), preferred_element_type=F32)
    density = jnp.sum(aux * f_ref[:rows, :].astype(F32), axis=0, keepdims=True)
    v_ext = jnp.concatenate([v_ref[pl.ds(h * ways + orb, 1), :] for h in range(planes)], axis=1)
    potential = v_ext + density / jnp.sqrt(1.0 + density * density)
    w_ref[...] = (f_ref[:rows, :].astype(F32) * potential).astype(BF16)
    blocks = lax.dot_general(w_ref[...], f_ref[:rows, :], contract, preferred_element_type=F32)
    own_out[...] = jnp.zeros_like(own_out)
    low_out[...] = jnp.zeros_like(low_out)
    for c in range(sources):
        own = own_ref[c]
        mine = jnp.concatenate(
            [blocks[(s * sources + c) * atoms : (s * sources + c + 1) * atoms] for s in range(functions)],
            axis=0,
        )
        high = mine.astype(BF16)
        low = (mine - high.astype(F32)).astype(BF16)
        both = jnp.concatenate([high, low], axis=0)
        for first, count, lanes in spans:
            cols = count * band
            spread = jnp.dot(
                both[:, first * band : first * band + cols],
                table_ref[c, :cols, :lanes],
                preferred_element_type=F32,
            )
            spread = spread[:block] + spread[block:]
            owned = jnp.concatenate([own] * (lanes // LANES), axis=1)
            picked = jnp.concatenate(
                [
                    jnp.sum(spread[s * atoms : (s + 1) * atoms] * owned, axis=0, keepdims=True)
                    for s in range(functions)
                ],
                axis=0,
            )
            place = pl.ds(first * pairs, lanes)
            if c < ways:
                own_out[c, :functions, place] = picked
            else:
                low_out[c - ways, :functions, place] = picked
        if c < ways:
            for h in range(planes):
                own_out[c, 16 + h : 17 + h, :points] = density[:, h * points : (h + 1) * points]


def final_kernel(dims, orb_ref, mine_ref, other_ref, *rest):
    _, functions, _, points, slab, ways, _, pairs, _ = dims
    planes = slab // ways
    message_refs = rest[:ways]
    density_out, blocks_out, density_ref, blocks_ref, pad_ref, sems = rest[ways:]
    orb = orb_ref[0]
    for k in range(ways):
        residue = lax.rem(orb + k, ways)
        for h in range(planes):
            density_ref[pl.ds(h * ways + residue, 1), :] = message_refs[k][16 + h : 17 + h, :points]
    first = pltpu.make_async_copy(density_ref, density_out, sems.at[0])
    first.start()
    total = mine_ref[...] + other_ref[...]
    per = LANES // pairs
    for t in range(functions):
        g, i = t // per, t % per
        piece = total[:, g * LANES : (g + 1) * LANES]
        if i:
            piece = pltpu.roll(piece, LANES - i * pairs, 1)
        pad_ref[t] = piece
    for t in range(functions):
        for s in range(functions):
            blocks_ref[s, t : t + 1, :] = pad_ref[t, s : s + 1, :pairs]
    second = pltpu.make_async_copy(blocks_ref, blocks_out, sems.at[1])
    second.start()
    first.wait()
    second.wait()


def on_device(support, anchor, kernel, pair_owner, pair_partner, pair_live, v_ext):
    atoms, functions, depth, points = support.shape
    pairs = kernel.shape[0]
    slab = v_ext.shape[0]
    ways = lax.axis_size("orb")
    space = lax.axis_size("space")
    planes = slab // ways
    reach = min((depth - 2) // ways + 1, planes)
    dims = (atoms, functions, depth, points, slab, ways, reach, pairs, space)
    orb = jnp.reshape(lax.axis_index("orb"), (1,)).astype(jnp.int32)
    domain = jnp.reshape(lax.axis_index("space"), (1,)).astype(jnp.int32)
    block = functions * atoms
    band = 2 * ways * atoms
    per = LANES // pairs
    groups = -(-functions // per)
    lanes = groups * LANES
    height = round_up(groups * functions + 3, 16)
    smem = pl.BlockSpec(memory_space=pltpu.SMEM)
    vmem = pl.BlockSpec(memory_space=pltpu.VMEM)
    hbm = pl.BlockSpec(memory_space=pltpu.HBM)

    packed = pl.pallas_call(
        functools.partial(pack_kernel, dims),
        out_shape=[jax.ShapeDtypeStruct((planes + 1, block, points), BF16)] * ways
        + [jax.ShapeDtypeStruct((reach + 1, block, points), BF16)] * ways,
        in_specs=[smem, smem] + [hbm] * 6,
        out_specs=[vmem] * (2 * ways),
        scratch_shapes=[
            pltpu.VMEM((functions, 16, LANES), F32),
            pltpu.VMEM((height, LANES), F32),
            pltpu.SMEM((atoms,), jnp.int32),
            pltpu.VMEM((functions, depth, atoms, points), BF16),
            pltpu.VMEM((functions, functions, pairs), F32),
            pltpu.VMEM((1, pairs), jnp.int32),
            pltpu.VMEM((1, pairs), jnp.int32),
            pltpu.VMEM((1, pairs), jnp.int32),
            pltpu.SemaphoreType.DMA((functions,)),
            pltpu.SemaphoreType.DMA((6,)),
        ],
        compiler_params=pltpu.CompilerParams(vmem_limit_bytes=8 << 20),
        name="pack",
    )(
        orb,
        domain,
        fixed(anchor),
        fixed(support.transpose(1, 2, 0, 3)),
        fixed(kernel.transpose(1, 2, 0)),
        fixed(pair_owner.reshape(1, pairs)),
        fixed(pair_partner.reshape(1, pairs)),
        fixed(pair_live.reshape(1, pairs)),
    )
    own, onward = packed[:ways], packed[ways:]
    upper, peers = [], []
    for k in range(ways):
        upper.append(moved_by(onward[k], ("space", "orb"), (1, k)))
    for k in range(1, ways):
        peers.append(moved_by(own[k], ("orb",), (k,)))
    sources = [own[0]] + peers + upper

    rows = functions * band
    padded = round_up(rows, LANES)
    most = 256 // max(band, pairs)
    own_part, low_part = pl.pallas_call(
        functools.partial(main_kernel, dims),
        out_shape=[
            jax.ShapeDtypeStruct((ways, 16 + round_up(planes, 8), lanes), F32),
            jax.ShapeDtypeStruct((ways, 16, lanes), F32),
        ],
        in_specs=[smem] + [vmem] * (1 + 2 * ways),
        out_specs=[vmem] * 2,
        scratch_shapes=[
            pltpu.VMEM((padded, planes * points), BF16),
            pltpu.VMEM((rows, planes * points), BF16),
            pltpu.VMEM((rows, 2 * padded), BF16),
            pltpu.VMEM((2 * ways, most * band, round_up(most * pairs, LANES)), BF16),
            pltpu.VMEM((2 * ways, atoms, LANES), F32),
            pltpu.VMEM((2 * height, LANES), F32),
        ],
        compiler_params=pltpu.CompilerParams(vmem_limit_bytes=24 << 20),
        name="main",
    )(orb, v_ext, *sources)

    from_above = moved_by(low_part, ("space",), (-1,))
    total = own_part + jnp.pad(from_above, ((0, 0), (0, own_part.shape[1] - 16), (0, 0)))
    messages = [total[0]]
    mine = total[0, :16]
    for k in range(1, ways):
        message = moved_by(total[k], ("orb",), (-k,))
        messages.append(message)
        mine = mine + message[:16]
    shares = lax.axis_size("grid")
    other = moved_by(mine, ("grid",), (1,))
    for k in range(2, shares):
        other = other + moved_by(mine, ("grid",), (k,))
    density, blocks = pl.pallas_call(
        functools.partial(final_kernel, dims),
        out_shape=[
            jax.ShapeDtypeStruct((slab, points), F32),
            jax.ShapeDtypeStruct((functions, functions, pairs), F32),
        ],
        in_specs=[smem] + [vmem] * (2 + ways),
        out_specs=[hbm] * 2,
        scratch_shapes=[
            pltpu.VMEM((slab, points), F32),
            pltpu.VMEM((functions, functions, pairs), F32),
            pltpu.VMEM((functions, 16, LANES), F32),
            pltpu.SemaphoreType.DMA((2,)),
        ],
        compiler_params=pltpu.CompilerParams(vmem_limit_bytes=4 << 20),
        name="final",
    )(orb, mine, other, *messages)
    return (density, blocks.transpose(2, 0, 1))


def solution(mesh):
    placed = (
        P(("shift", "space", "orb"), None, None, "grid"),
        P(("shift", "space", "orb")),
        P(("shift", "space", "orb"), None, None),
        P(("shift", "space", "orb")),
        P(("shift", "space", "orb")),
        P(("shift", "space", "orb")),
        P(("shift", "space"), "grid"),
    )
    return jax.shard_map(
        on_device,
        mesh=mesh,
        in_specs=placed,
        out_specs=(P(("shift", "space"), "grid"), P(("shift", "space", "orb"), None, None)),
        check_vma=False,
    )
```

```python
import functools

import jax
import jax.numpy as jnp
from jax import lax
from jax.experimental import pallas as pl
from jax.experimental.pallas import tpu as pltpu
from jax.sharding import PartitionSpec as P


LANES = 128
F32 = jnp.float32
BF16 = jnp.bfloat16


def moved_by(value, axes, steps):
    sizes = [lax.axis_size(axis) for axis in axes]
    pairs = []
    total = 1
    for size in sizes:
        total *= size
    for source in range(total):
        rest, place = source, []
        for size in reversed(sizes):
            place.insert(0, rest % size)
            rest //= size
        target = 0
        for size, here, step in zip(sizes, place, steps):
            target = target * size + (here + step) % size
        pairs.append((source, target))
    return lax.ppermute(value, axes if len(axes) > 1 else axes[0], pairs)


def round_up(count, unit):
    return (count + unit - 1) // unit * unit


def fixed(value):
    return pltpu.with_memory_space_constraint(value, pltpu.HBM)


def pack_kernel(dims, orb_ref, domain_ref, *rest):
    atoms, functions, depth, points, slab, ways, reach, pairs, space = dims
    given, rest = rest[:6], rest[6:]
    own_refs, next_refs = rest[:ways], rest[ways : 2 * ways]
    k_pad, row_pad, *held, x_sem, sems = rest[2 * ways :]
    anchor_ref, x_ref, k_ref, owner_ref, partner_ref, live_ref = held
    copies = [
        pltpu.make_async_copy(given[i], held[i], sems.at[i]) for i in range(6) if i != 1
    ]
    x_copies = [
        pltpu.make_async_copy(given[1].at[s], x_ref.at[s], x_sem.at[s]) for s in range(functions)
    ]
    copies[0].start()
    for copy in x_copies:
        copy.start()
    for copy in copies[1:]:
        copy.start()
    copies[0].wait()
    planes = slab // ways
    boxes = -(-depth // ways)
    orb, domain = orb_ref[0], domain_ref[0]
    atom = lax.broadcasted_iota(jnp.int32, (atoms, points), 0)
    offset = jnp.zeros((atoms, points), jnp.int32)
    for a in range(atoms):
        offset = jnp.where(atom == a, lax.rem(anchor_ref[a], slab), offset)
    zero = jnp.zeros((atoms, points), F32)
    masks = []
    for k in range(ways):
        residue = lax.rem(orb + k, ways)
        start = offset - residue
        shift = jnp.zeros((atoms, points), jnp.int32)
        for low in range(slab // ways):
            shift = shift + (start > low * ways).astype(jnp.int32)
        phase = shift * ways - start
        bits, size = [], 1
        while size <= -(-(slab - 1) // ways):
            bits.append((size, (shift & size) != 0))
            size *= 2
        masks.append(([phase == e for e in range(ways)], bits))
    for s in range(functions):
        x_copies[s].wait()
        tiles = [x_ref[s, j].astype(F32) for j in range(depth)]
        for k in range(ways):
            phases, bits = masks[k]
            line = []
            for m in range(boxes):
                pick = zero
                for e in range(ways):
                    j = m * ways + e
                    pick = jnp.where(phases[e], tiles[j] if j < depth else zero, pick)
                line.append(pick)
            for size, mask in bits:
                length = min(len(line) + size, planes + reach)
                line = [
                    jnp.where(
                        mask,
                        line[h - size] if h >= size else zero,
                        line[h] if h < len(line) else zero,
                    )
                    for h in range(length)
                ]
            line = line + [zero] * (planes + reach - len(line))
            rows = pl.ds(s * atoms, atoms)
            for h in range(planes):
                own_refs[k][h, rows, :] = line[h].astype(BF16)
            for h in range(reach):
                next_refs[k][h, rows, :] = line[planes + h].astype(BF16)
    per = LANES // pairs
    groups = -(-functions // per)
    for copy in copies[1:]:
        copy.wait()
    k_pad[...] = jnp.zeros_like(k_pad)
    k_pad[:, :functions, :pairs] = k_ref[...]
    row_pad[...] = jnp.zeros_like(row_pad)
    for s in range(functions):
        for g in range(groups):
            row = jnp.zeros((1, LANES), F32)
            for i in range(per):
                t = g * per + i
                if t < functions:
                    piece = k_pad[s, t : t + 1, :]
                    row = row + (pltpu.roll(piece, i * pairs, 1) if i else piece)
            row_pad[g * functions + s : g * functions + s + 1, :] = row
    per_domain = atoms * ways
    owner = owner_ref[...] - (domain * ways + orb) * atoms
    partner = partner_ref[...]
    home = jnp.floor((partner.astype(F32) + 0.5) * (1.0 / per_domain)).astype(jnp.int32)
    relative = home - domain + 1
    relative = jnp.where(relative < 0, relative + space, relative)
    relative = jnp.where(relative >= space, relative - space, relative)
    code = relative * per_domain + partner - home * per_domain
    base = groups * functions
    row_pad[base : base + 1, :pairs] = owner.astype(F32)
    row_pad[base + 1 : base + 2, :pairs] = live_ref[...].astype(F32)
    row_pad[base + 2 : base + 3, :pairs] = code.astype(F32)
    index = row_pad[base : base + 3, :]
    wide = index
    for i in range(1, per):
        wide = wide + pltpu.roll(index, i * pairs, 1)
    row_pad[base : base + 3, :] = wide
    info = row_pad[...]
    high = info.astype(BF16)
    low = (info - high.astype(F32)).astype(BF16)
    height = info.shape[0]
    for refs, last in ((own_refs, planes), (next_refs, reach)):
        for k in range(ways):
            refs[k][last, 0:height, :] = high
            refs[k][last, height : 2 * height, :] = low


def main_kernel(dims, orb_ref, v_ref, *rest):
    atoms, functions, _, points, slab, ways, _, pairs, _ = dims
    planes = slab // ways
    sources = 2 * ways
    source_refs = rest[:sources]
    own_outs, low_outs = rest[sources : sources + ways], rest[sources + ways : sources + 2 * ways]
    f_ref, w_ref, d_ref, table_ref, own_ref, info_ref = rest[sources + 2 * ways :]
    block = functions * atoms
    band = sources * atoms
    rows = functions * band
    padded = f_ref.shape[0]
    per = LANES // pairs
    groups = -(-functions // per)
    height = info_ref.shape[0] // 2
    spans, first = [], 0
    most = table_ref.shape[1] // band
    while first < functions:
        count = min(most, functions - first)
        spans.append((first, count, round_up(count * pairs, LANES)))
        first += count
    orb = orb_ref[0]
    per_domain = atoms * ways
    contract = (((1,), (1,)), ((), ()))
    for h in range(planes):
        for c in range(sources):
            last = source_refs[c].shape[0] - 1
            for s in range(functions):
                place = (pl.ds((s * sources + c) * atoms, atoms), pl.ds(h * points, points))
                if h < last:
                    f_ref[place] = source_refs[c][h, s * atoms : (s + 1) * atoms, :]
                else:
                    f_ref[place] = jnp.zeros((atoms, points), BF16)
    if padded > rows:
        f_ref[rows:, :] = jnp.zeros((padded - rows, planes * points), BF16)
    tail = rows // LANES * LANES
    if padded > tail:
        d_ref[:, tail:padded] = jnp.zeros((rows, padded - tail), BF16)
        d_ref[:, padded + tail :] = jnp.zeros((rows, padded - tail), BF16)
    size = table_ref.shape[1:]
    row_id = lax.broadcasted_iota(jnp.int32, size, 0)
    lane_id = lax.broadcasted_iota(jnp.int32, (1, size[1]), 1)
    function_id = jnp.zeros((1, size[1]), jnp.int32)
    for t in range(1, size[1] // pairs):
        function_id = function_id + (lane_id >= t * pairs).astype(jnp.int32)
    atom_id = lax.broadcasted_iota(jnp.int32, (atoms, LANES), 0)
    base = groups * functions
    for c in range(sources):
        last = source_refs[c].shape[0] - 1
        pair_high = source_refs[c][last, 0:height, :].astype(F32)
        pair_low = source_refs[c][last, height : 2 * height, :].astype(F32)
        owner = pair_high[base : base + 1, :].astype(jnp.int32)
        live = pair_high[base + 1 : base + 2, :]
        code = pair_high[base + 2 : base + 3, :].astype(jnp.int32)
        domain = (code >= per_domain).astype(jnp.int32) + (code >= 2 * per_domain).astype(jnp.int32)
        inside = code - domain * per_domain
        orb_of = jnp.zeros(code.shape, jnp.int32)
        for i in range(1, ways):
            orb_of = orb_of + (inside >= i * atoms).astype(jnp.int32)
        local = inside - orb_of * atoms
        slot = orb - orb_of
        slot = jnp.where(slot < 0, slot + ways, slot)
        if c < ways:
            slot = slot + jnp.where(domain == 0, ways, 0)
            valid = domain <= 1
        else:
            slot = slot + jnp.where(domain == 1, ways, 0)
            valid = domain >= 1
        inner = jnp.where(valid, slot * atoms + local, -padded * LANES)
        inner = jnp.concatenate([inner] * (size[1] // LANES), axis=1)
        target = inner + function_id * band
        table = jnp.where(row_id == target, 1.0, 0.0).astype(BF16)
        table_ref[c] = table
        own = jnp.where(atom_id == owner, live, 0.0)
        own_ref[c] = own
        for first, count, lanes in spans:
            parts = []
            for pair_rows in (pair_high, pair_low):
                for s in range(functions):
                    parts.append(
                        jnp.concatenate(
                            [
                                pair_rows[g * functions + s : g * functions + s + 1, :] * own
                                for g in range(first // per, first // per + lanes // LANES)
                            ],
                            axis=1,
                        )
                    )
            left = jnp.concatenate(parts, axis=0).astype(BF16)
            cols = count * band
            part = lax.dot_general(
                left, table_ref[c, :cols, :lanes], contract, preferred_element_type=F32
            )
            part = part[:block] + part[block:]
            high = part.astype(BF16)
            low = (part - high.astype(F32)).astype(BF16)
            for s in range(functions):
                place = pl.ds((s * sources + c) * atoms, atoms)
                d_ref[place, first * band : first * band + cols] = high[s * atoms : (s + 1) * atoms]
                d_ref[place, padded + first * band : padded + first * band + cols] = low[
                    s * atoms : (s + 1) * atoms
                ]
    f_all = f_ref[...]
    aux = jnp.dot(d_ref[...], jnp.concatenate([f_all, f_all], axis=0), preferred_element_type=F32)
    density = jnp.sum(aux * f_ref[:rows, :].astype(F32), axis=0, keepdims=True)
    v_ext = jnp.concatenate([v_ref[pl.ds(h * ways + orb, 1), :] for h in range(planes)], axis=1)
    potential = v_ext + density / jnp.sqrt(1.0 + density * density)
    w_ref[...] = (f_ref[:rows, :].astype(F32) * potential).astype(BF16)
    blocks = lax.dot_general(w_ref[...], f_ref[:rows, :], contract, preferred_element_type=F32)
    used = groups * functions
    head = round_up(used, 8)
    for out in (*own_outs, *low_outs):
        out[used:, :] = jnp.zeros((out.shape[0] - used, LANES), F32)
    for c in range(sources):
        own = own_ref[c]
        mine = jnp.concatenate(
            [blocks[(s * sources + c) * atoms : (s * sources + c + 1) * atoms] for s in range(functions)],
            axis=0,
        )
        high = mine.astype(BF16)
        low = (mine - high.astype(F32)).astype(BF16)
        both = jnp.concatenate([high, low], axis=0)
        for first, count, lanes in spans:
            cols = count * band
            spread = jnp.dot(
                both[:, first * band : first * band + cols],
                table_ref[c, :cols, :lanes],
                preferred_element_type=F32,
            )
            spread = spread[:block] + spread[block:]
            owned = jnp.concatenate([own] * (lanes // LANES), axis=1)
            picked = jnp.concatenate(
                [
                    jnp.sum(spread[s * atoms : (s + 1) * atoms] * owned, axis=0, keepdims=True)
                    for s in range(functions)
                ],
                axis=0,
            )
            out = own_outs[c] if c < ways else low_outs[c - ways]
            for i in range(lanes // LANES):
                g = first // per + i
                out[g * functions : (g + 1) * functions, :] = picked[:, i * LANES : (i + 1) * LANES]
        if c < ways:
            for h in range(planes):
                own_outs[c][head + h : head + h + 1, :points] = density[
                    :, h * points : (h + 1) * points
                ]


def final_kernel(dims, orb_ref, mine_ref, other_ref, *rest):
    _, functions, _, points, slab, ways, _, pairs, _ = dims
    planes = slab // ways
    message_refs = rest[:ways]
    density_out, blocks_out, density_ref, blocks_ref, pad_ref, sems = rest[ways:]
    orb = orb_ref[0]
    per = LANES // pairs
    groups = -(-functions // per)
    head = round_up(groups * functions, 8)
    for k in range(ways):
        residue = lax.rem(orb + k, ways)
        for h in range(planes):
            density_ref[pl.ds(h * ways + residue, 1), :] = message_refs[k][
                head + h : head + h + 1, :points
            ]
    first = pltpu.make_async_copy(density_ref, density_out, sems.at[0])
    first.start()
    total = mine_ref[...] + other_ref[...]
    for t in range(functions):
        g, i = t // per, t % per
        piece = total[g * functions : (g + 1) * functions]
        if i:
            piece = pltpu.roll(piece, LANES - i * pairs, 1)
        pad_ref[t] = piece
    for t in range(functions):
        for s in range(functions):
            blocks_ref[s, t : t + 1, :] = pad_ref[t, s : s + 1, :pairs]
    second = pltpu.make_async_copy(blocks_ref, blocks_out, sems.at[1])
    second.start()
    first.wait()
    second.wait()


def on_device(support, anchor, kernel, pair_owner, pair_partner, pair_live, v_ext):
    atoms, functions, depth, points = support.shape
    pairs = kernel.shape[0]
    slab = v_ext.shape[0]
    ways = lax.axis_size("orb")
    space = lax.axis_size("space")
    planes = slab // ways
    reach = min((depth - 2) // ways + 1, planes)
    dims = (atoms, functions, depth, points, slab, ways, reach, pairs, space)
    orb = jnp.reshape(lax.axis_index("orb"), (1,)).astype(jnp.int32)
    domain = jnp.reshape(lax.axis_index("space"), (1,)).astype(jnp.int32)
    block = functions * atoms
    band = 2 * ways * atoms
    per = LANES // pairs
    groups = -(-functions // per)
    height = round_up(groups * functions + 3, 16)
    smem = pl.BlockSpec(memory_space=pltpu.SMEM)
    vmem = pl.BlockSpec(memory_space=pltpu.VMEM)
    hbm = pl.BlockSpec(memory_space=pltpu.HBM)

    packed = pl.pallas_call(
        functools.partial(pack_kernel, dims),
        out_shape=[jax.ShapeDtypeStruct((planes + 1, block, points), BF16)] * ways
        + [jax.ShapeDtypeStruct((reach + 1, block, points), BF16)] * ways,
        in_specs=[smem, smem] + [hbm] * 6,
        out_specs=[vmem] * (2 * ways),
        scratch_shapes=[
            pltpu.VMEM((functions, 16, LANES), F32),
            pltpu.VMEM((height, LANES), F32),
            pltpu.SMEM((atoms,), jnp.int32),
            pltpu.VMEM((functions, depth, atoms, points), BF16),
            pltpu.VMEM((functions, functions, pairs), F32),
            pltpu.VMEM((1, pairs), jnp.int32),
            pltpu.VMEM((1, pairs), jnp.int32),
            pltpu.VMEM((1, pairs), jnp.int32),
            pltpu.SemaphoreType.DMA((functions,)),
            pltpu.SemaphoreType.DMA((6,)),
        ],
        compiler_params=pltpu.CompilerParams(vmem_limit_bytes=8 << 20),
        name="pack",
    )(
        orb,
        domain,
        fixed(anchor),
        fixed(support.transpose(1, 2, 0, 3)),
        fixed(kernel.transpose(1, 2, 0)),
        fixed(pair_owner.reshape(1, pairs)),
        fixed(pair_partner.reshape(1, pairs)),
        fixed(pair_live.reshape(1, pairs)),
    )
    own, onward = packed[:ways], packed[ways:]
    upper, peers = [], []
    for k in range(ways):
        upper.append(moved_by(onward[k], ("space", "orb"), (1, k)))
    for k in range(1, ways):
        peers.append(moved_by(own[k], ("orb",), (k,)))
    sources = [own[0]] + peers + upper

    rows = functions * band
    padded = round_up(rows, LANES)
    most = 256 // max(band, pairs)
    head = round_up(groups * functions, 8)
    parts = pl.pallas_call(
        functools.partial(main_kernel, dims),
        out_shape=[jax.ShapeDtypeStruct((head + round_up(planes, 8), LANES), F32)] * ways
        + [jax.ShapeDtypeStruct((head, LANES), F32)] * ways,
        in_specs=[smem] + [vmem] * (1 + 2 * ways),
        out_specs=[vmem] * (2 * ways),
        scratch_shapes=[
            pltpu.VMEM((padded, planes * points), BF16),
            pltpu.VMEM((rows, planes * points), BF16),
            pltpu.VMEM((rows, 2 * padded), BF16),
            pltpu.VMEM((2 * ways, most * band, round_up(most * pairs, LANES)), BF16),
            pltpu.VMEM((2 * ways, atoms, LANES), F32),
            pltpu.VMEM((2 * height, LANES), F32),
        ],
        compiler_params=pltpu.CompilerParams(vmem_limit_bytes=24 << 20),
        name="main",
    )(orb, v_ext, *sources)

    own_parts, low_parts = parts[:ways], parts[ways:]
    messages, arrived = [own_parts[0]], []
    for k in range(ways):
        arrived.append(moved_by(low_parts[k], ("space", "orb"), (-1, -k)))
    for k in range(1, ways):
        messages.append(moved_by(own_parts[k], ("orb",), (-k,)))
    mine = arrived[0]
    for part in arrived[1:]:
        mine = mine + part
    for message in messages:
        mine = mine + message[:head]
    shares = lax.axis_size("grid")
    other = moved_by(mine, ("grid",), (1,))
    for k in range(2, shares):
        other = other + moved_by(mine, ("grid",), (k,))
    density, blocks = pl.pallas_call(
        functools.partial(final_kernel, dims),
        out_shape=[
            jax.ShapeDtypeStruct((slab, points), F32),
            jax.ShapeDtypeStruct((functions, functions, pairs), F32),
        ],
        in_specs=[smem] + [vmem] * (2 + ways),
        out_specs=[hbm] * 2,
        scratch_shapes=[
            pltpu.VMEM((slab, points), F32),
            pltpu.VMEM((functions, functions, pairs), F32),
            pltpu.VMEM((functions, functions, LANES), F32),
            pltpu.SemaphoreType.DMA((2,)),
        ],
        compiler_params=pltpu.CompilerParams(vmem_limit_bytes=4 << 20),
        name="final",
    )(orb, mine, other, *messages)
    return (density, blocks.transpose(2, 0, 1))


def solution(mesh):
    placed = (
        P(("shift", "space", "orb"), None, None, "grid"),
        P(("shift", "space", "orb")),
        P(("shift", "space", "orb"), None, None),
        P(("shift", "space", "orb")),
        P(("shift", "space", "orb")),
        P(("shift", "space", "orb")),
        P(("shift", "space"), "grid"),
    )
    return jax.shard_map(
        on_device,
        mesh=mesh,
        in_specs=placed,
        out_specs=(P(("shift", "space"), "grid"), P(("shift", "space", "orb"), None, None)),
        check_vma=False,
    )
```

```python
import functools

import jax
import jax.numpy as jnp
from jax import lax
from jax.experimental import pallas as pl
from jax.experimental.pallas import tpu as pltpu
from jax.sharding import PartitionSpec as P


LANES = 128
F32 = jnp.float32
BF16 = jnp.bfloat16


def moved_by(value, axes, steps):
    sizes = [lax.axis_size(axis) for axis in axes]
    pairs = []
    total = 1
    for size in sizes:
        total *= size
    for source in range(total):
        rest, place = source, []
        for size in reversed(sizes):
            place.insert(0, rest % size)
            rest //= size
        target = 0
        for size, here, step in zip(sizes, place, steps):
            target = target * size + (here + step) % size
        pairs.append((source, target))
    return lax.ppermute(value, axes if len(axes) > 1 else axes[0], pairs)


def round_up(count, unit):
    return (count + unit - 1) // unit * unit


def fixed(value):
    return pltpu.with_memory_space_constraint(value, pltpu.HBM)


def pieces_of(functions, pairs):
    per = LANES // pairs
    full = functions // per * per
    places = {}
    for t in range(full):
        for s in range(functions):
            places[t, s] = (t // per * functions + s, t % per)
    count = full * functions
    for t in range(full, functions):
        for s in range(functions):
            places[t, s] = (count // per, count % per)
            count += 1
    for name in range(3):
        places[name] = (count // per, count % per)
        count += 1
    return places, round_up(-(-count // per), 8)


def plane_masks(atoms, points, slab, ways, repeat, anchor_ref, residues):
    rows = atoms * repeat
    row = lax.broadcasted_iota(jnp.int32, (rows, points), 0)
    offset = jnp.zeros((rows, points), jnp.int32)
    for a in range(atoms):
        here = row == a
        for i in range(1, repeat):
            here = here | (row == a + i * atoms)
        offset = jnp.where(here, lax.rem(anchor_ref[a], slab), offset)
    planes = slab // ways
    found = []
    for residue in residues:
        start = offset - residue
        shift = jnp.zeros((rows, points), jnp.int32)
        for low in range(planes):
            shift = shift + (start > low * ways).astype(jnp.int32)
        phase = (shift * ways - start).astype(F32).astype(BF16)
        bits, size = [], 1
        while size <= planes:
            if size % planes:
                bit = ((shift & size) != 0).astype(F32).astype(BF16)
                bits.append((size, bit > 0.5))
            size *= 2
        level = shift.astype(F32).astype(BF16)
        found.append(
            (
                [phase == float(e) for e in range(ways - 1)],
                bits,
                [level <= float(h) for h in range(planes)],
            )
        )
    return found


def pack_kernel(dims, *rest):
    atoms, functions, depth, points, slab, ways, reach, pairs, space = dims
    given, rest = rest[:6], rest[6:]
    own_refs, next_refs = rest[:ways], rest[ways : 2 * ways]
    k_pad, row_pad, *held, x_sem, sems = rest[2 * ways :]
    anchor_ref, x_ref, k_ref, owner_ref, partner_ref, live_ref = held
    block = functions * atoms
    copies = [
        pltpu.make_async_copy(given[i], held[i], sems.at[i]) for i in range(6) if i != 1
    ]
    x_copies = [
        pltpu.make_async_copy(
            given[1].at[s], x_ref.at[:, pl.ds(s * atoms, atoms), :], x_sem.at[s]
        )
        for s in range(functions)
    ]
    copies[0].start()
    for copy in x_copies:
        copy.start()
    for copy in copies[1:]:
        copy.start()
    k_pad[...] = jnp.zeros_like(k_pad)
    row_pad[...] = jnp.zeros_like(row_pad)
    planes = slab // ways
    orb, domain = lax.axis_index("orb"), lax.axis_index("space")
    copies[0].wait()
    residues = [lax.rem(orb + k, ways) for k in range(ways)]
    first = 0
    masks = {}
    while first < functions:
        repeat = min(2, functions - first)
        if repeat not in masks:
            masks[repeat] = plane_masks(atoms, points, slab, ways, repeat, anchor_ref, residues)
        for s in range(first, first + repeat):
            x_copies[s].wait()
        rows = atoms * repeat
        zero = jnp.zeros((rows, points), BF16)
        tiles = [x_ref[j, first * atoms : first * atoms + rows, :] for j in range(depth)]
        tiles = tiles + [zero] * (planes * ways - depth)
        for k in range(ways):
            phases, bits, levels = masks[repeat][k]
            line = []
            for m in range(planes):
                pick = tiles[m * ways + ways - 1]
                for e in reversed(range(ways - 1)):
                    pick = jnp.where(phases[e], tiles[m * ways + e], pick)
                line.append(pick)
            for size, mask in bits:
                line = [jnp.where(mask, line[(h - size) % planes], line[h]) for h in range(planes)]
            for h in range(planes):
                place = h * block + first * atoms
                own_refs[k][place : place + rows, :] = jnp.where(levels[h], line[h], zero)
                if h < reach:
                    next_refs[k][place : place + rows, :] = jnp.where(levels[h], zero, line[h])
        first += repeat
    for copy in copies[1:]:
        copy.wait()
    places, height = pieces_of(functions, pairs)
    k_pad[0:functions, :functions, :pairs] = k_ref[...]
    per_domain = atoms * ways
    owner = owner_ref[...] - (domain * ways + orb) * atoms
    partner = partner_ref[...]
    home = jnp.floor((partner.astype(F32) + 0.5) * (1.0 / per_domain)).astype(jnp.int32)
    relative = home - domain + 1
    relative = jnp.where(relative < 0, relative + space, relative)
    relative = jnp.where(relative >= space, relative - space, relative)
    code = relative * per_domain + partner - home * per_domain
    k_pad[functions, 0:1, :pairs] = owner.astype(F32)
    k_pad[functions, 1:2, :pairs] = live_ref[...].astype(F32)
    k_pad[functions, 2:3, :pairs] = code.astype(F32)
    lines = {}
    for name, (row, column) in places.items():
        if isinstance(name, tuple):
            piece = k_pad[name[1], name[0] : name[0] + 1, :]
        else:
            piece = k_pad[functions, name : name + 1, :]
        piece = pltpu.roll(piece, column * pairs, 1) if column else piece
        lines[row] = lines[row] + piece if row in lines else piece
    for row, line in lines.items():
        row_pad[row : row + 1, :] = line
    info = row_pad[...]
    high = info.astype(BF16)
    low = (info - high.astype(F32)).astype(BF16)
    for refs, last in ((own_refs, planes), (next_refs, reach)):
        for k in range(ways):
            refs[k][last * block : last * block + height, :] = high
            refs[k][last * block + height : last * block + 2 * height, :] = low


def spans_of(functions, pairs, band):
    most = 256 // max(band, pairs)
    spans, first = [], 0
    while first < functions:
        count = min(most, functions - first)
        spans.append((first, count, round_up(count * pairs, LANES)))
        first += count
    return spans, (most * band, round_up(most * pairs, LANES))


def lined(rows, place, pairs):
    row, column = place
    line = rows[row : row + 1, :]
    return pltpu.roll(line, LANES - column * pairs, 1) if column else line


def fill_source(dims, c, source_ref, f_ref, d_ref, table_ref, own_ref):
    atoms, functions, _, points, slab, ways, _, pairs, _ = dims
    orb = lax.axis_index("orb")
    planes = slab // ways
    sources = 2 * ways
    block = functions * atoms
    band = sources * atoms
    padded = f_ref.shape[0]
    per = LANES // pairs
    places, height = pieces_of(functions, pairs)
    spans, size = spans_of(functions, pairs, band)
    per_domain = atoms * ways
    contract = (((1,), (1,)), ((), ()))
    last = (source_ref.shape[0] - 2 * height) // block
    for h in range(planes):
        for s in range(functions):
            place = (pl.ds((s * sources + c) * atoms, atoms), pl.ds(h * points, points))
            if h < last:
                f_ref[place] = source_ref[h * block + s * atoms : h * block + (s + 1) * atoms, :]
            else:
                f_ref[place] = jnp.zeros((atoms, points), BF16)
    row_id = lax.broadcasted_iota(jnp.int32, size, 0)
    lane_id = lax.broadcasted_iota(jnp.int32, (1, size[1]), 1)
    function_id = jnp.zeros((1, size[1]), jnp.int32)
    for t in range(1, size[1] // pairs):
        function_id = function_id + (lane_id >= t * pairs).astype(jnp.int32)
    atom_id = lax.broadcasted_iota(jnp.int32, (atoms, LANES), 0)
    pair_high = source_ref[last * block : last * block + height, :].astype(F32)
    pair_low = source_ref[last * block + height : last * block + 2 * height, :].astype(F32)
    row_lane = lax.broadcasted_iota(jnp.int32, (1, LANES), 1)
    wide = []
    for name in range(3):
        row, column = places[name]
        piece = pair_high[row : row + 1, :]
        piece = jnp.where(
            (row_lane >= column * pairs) & (row_lane < (column + 1) * pairs), piece, 0.0
        )
        line = piece
        for i in range(1, per):
            line = line + pltpu.roll(piece, i * pairs, 1)
        wide.append(line)
    owner, live, code = wide[0].astype(jnp.int32), wide[1], wide[2].astype(jnp.int32)
    domain = (code >= per_domain).astype(jnp.int32) + (code >= 2 * per_domain).astype(jnp.int32)
    inside = code - domain * per_domain
    orb_of = jnp.zeros(code.shape, jnp.int32)
    for i in range(1, ways):
        orb_of = orb_of + (inside >= i * atoms).astype(jnp.int32)
    local = inside - orb_of * atoms
    slot = orb - orb_of
    slot = jnp.where(slot < 0, slot + ways, slot)
    if c < ways:
        slot = slot + jnp.where(domain == 0, ways, 0)
        valid = domain <= 1
    else:
        slot = slot + jnp.where(domain == 1, ways, 0)
        valid = domain >= 1
    inner = jnp.where(valid, slot * atoms + local, -padded * LANES)
    inner = jnp.concatenate([inner] * (size[1] // LANES), axis=1)
    target = inner + function_id * band
    table_ref[c] = jnp.where(row_id == target, 1.0, 0.0).astype(BF16)
    own = jnp.where(atom_id == owner, live, 0.0)
    own_ref[c] = own
    for first, count, lanes in spans:
        parts = []
        for pair_rows in (pair_high, pair_low):
            for s in range(functions):
                parts.append(
                    jnp.concatenate(
                        [
                            lined(pair_rows, places[g * per, s], pairs) * own
                            for g in range(first // per, first // per + lanes // LANES)
                        ],
                        axis=1,
                    )
                )
        left = jnp.concatenate(parts, axis=0).astype(BF16)
        cols = count * band
        part = lax.dot_general(
            left, table_ref[c, :cols, :lanes], contract, preferred_element_type=F32
        )
        part = part[:block] + part[block:]
        high = part.astype(BF16)
        low = (part - high.astype(F32)).astype(BF16)
        for s in range(functions):
            place = pl.ds((s * sources + c) * atoms, atoms)
            d_ref[place, first * band : first * band + cols] = high[s * atoms : (s + 1) * atoms]
            d_ref[place, padded + first * band : padded + first * band + cols] = low[
                s * atoms : (s + 1) * atoms
            ]


def first_kernel(dims, source_ref, f_ref, d_ref, table_ref, own_ref):
    rows, padded = d_ref.shape[0], f_ref.shape[0]
    if padded > rows:
        f_ref[rows:, :] = jnp.zeros((padded - rows, f_ref.shape[1]), BF16)
    tail = rows // LANES * LANES
    if padded > tail:
        d_ref[:, tail:padded] = jnp.zeros((rows, padded - tail), BF16)
        d_ref[:, padded + tail :] = jnp.zeros((rows, padded - tail), BF16)
    fill_source(dims, 0, source_ref, f_ref, d_ref, table_ref, own_ref)


def next_kernel(dims, c, source_ref, *rest):
    fill_source(dims, c, source_ref, *rest[4:])


def main_kernel(dims, c, v_ref, source_ref, *rest):
    atoms, functions, _, points, slab, ways, _, pairs, _ = dims
    planes = slab // ways
    sources = 2 * ways
    rest = rest[4:]
    own_outs, low_outs = rest[:ways], rest[ways : 2 * ways]
    f_ref, d_ref, table_ref, own_ref, w_ref = rest[2 * ways :]
    block = functions * atoms
    band = sources * atoms
    rows = functions * band
    per = LANES // pairs
    groups = -(-functions // per)
    spans, _ = spans_of(functions, pairs, band)
    orb = lax.axis_index("orb")
    contract = (((1,), (1,)), ((), ()))
    fill_source(dims, c, source_ref, f_ref, d_ref, table_ref, own_ref)
    f_all = f_ref[...]
    aux = jnp.dot(d_ref[...], jnp.concatenate([f_all, f_all], axis=0), preferred_element_type=F32)
    density = jnp.sum(aux * f_ref[:rows, :].astype(F32), axis=0, keepdims=True)
    v_ext = jnp.concatenate([v_ref[pl.ds(h * ways + orb, 1), :] for h in range(planes)], axis=1)
    potential = v_ext + density / jnp.sqrt(1.0 + density * density)
    w_ref[...] = (f_ref[:rows, :].astype(F32) * potential).astype(BF16)
    blocks = lax.dot_general(w_ref[...], f_ref[:rows, :], contract, preferred_element_type=F32)
    used = groups * functions
    head = round_up(used, 8)
    for out in (*own_outs, *low_outs):
        out[used:, :] = jnp.zeros((out.shape[0] - used, LANES), F32)
    for c in range(sources):
        own = own_ref[c]
        mine = jnp.concatenate(
            [blocks[(s * sources + c) * atoms : (s * sources + c + 1) * atoms] for s in range(functions)],
            axis=0,
        )
        high = mine.astype(BF16)
        low = (mine - high.astype(F32)).astype(BF16)
        both = jnp.concatenate([high, low], axis=0)
        for first, count, lanes in spans:
            cols = count * band
            spread = jnp.dot(
                both[:, first * band : first * band + cols],
                table_ref[c, :cols, :lanes],
                preferred_element_type=F32,
            )
            spread = spread[:block] + spread[block:]
            owned = jnp.concatenate([own] * (lanes // LANES), axis=1)
            picked = jnp.concatenate(
                [
                    jnp.sum(spread[s * atoms : (s + 1) * atoms] * owned, axis=0, keepdims=True)
                    for s in range(functions)
                ],
                axis=0,
            )
            out = own_outs[c] if c < ways else low_outs[c - ways]
            for i in range(lanes // LANES):
                g = first // per + i
                out[g * functions : (g + 1) * functions, :] = picked[:, i * LANES : (i + 1) * LANES]
        if c < ways:
            for h in range(planes):
                own_outs[c][head + h : head + h + 1, :points] = density[
                    :, h * points : (h + 1) * points
                ]


def final_kernel(dims, mine_ref, other_ref, *rest):
    _, functions, _, points, slab, ways, _, pairs, _ = dims
    planes = slab // ways
    message_refs = rest[:ways]
    density_out, blocks_out, density_ref, blocks_ref, pad_ref, sems = rest[ways:]
    orb = lax.axis_index("orb")
    per = LANES // pairs
    groups = -(-functions // per)
    head = round_up(groups * functions, 8)
    for k in range(ways):
        residue = lax.rem(orb + k, ways)
        for h in range(planes):
            density_ref[pl.ds(h * ways + residue, 1), :] = message_refs[k][
                head + h : head + h + 1, :points
            ]
    first = pltpu.make_async_copy(density_ref, density_out, sems.at[0])
    first.start()
    total = mine_ref[...] + other_ref[...]
    for t in range(functions):
        g, i = t // per, t % per
        piece = total[g * functions : (g + 1) * functions]
        if i:
            piece = pltpu.roll(piece, LANES - i * pairs, 1)
        pad_ref[t] = piece
    for t in range(functions):
        for s in range(functions):
            blocks_ref[s, t : t + 1, :] = pad_ref[t, s : s + 1, :pairs]
    second = pltpu.make_async_copy(blocks_ref, blocks_out, sems.at[1])
    second.start()
    first.wait()
    second.wait()


def on_device(support, anchor, kernel, pair_owner, pair_partner, pair_live, v_ext):
    atoms, functions, depth, points = support.shape
    pairs = kernel.shape[0]
    slab = v_ext.shape[0]
    ways = lax.axis_size("orb")
    space = lax.axis_size("space")
    planes = slab // ways
    reach = min((depth - 2) // ways + 1, planes)
    dims = (atoms, functions, depth, points, slab, ways, reach, pairs, space)
    block = functions * atoms
    band = 2 * ways * atoms
    per = LANES // pairs
    groups = -(-functions // per)
    height = pieces_of(functions, pairs)[1]
    vmem = pl.BlockSpec(memory_space=pltpu.VMEM)
    hbm = pl.BlockSpec(memory_space=pltpu.HBM)

    packed = pl.pallas_call(
        functools.partial(pack_kernel, dims),
        out_shape=[jax.ShapeDtypeStruct((planes * block + 2 * height, points), BF16)] * ways
        + [jax.ShapeDtypeStruct((reach * block + 2 * height, points), BF16)] * ways,
        in_specs=[hbm] * 6,
        out_specs=[vmem] * (2 * ways),
        scratch_shapes=[
            pltpu.VMEM((functions + 1, 16, LANES), F32),
            pltpu.VMEM((height, LANES), F32),
            pltpu.SMEM((atoms,), jnp.int32),
            pltpu.VMEM((depth, block, points), BF16),
            pltpu.VMEM((functions, functions, pairs), F32),
            pltpu.VMEM((1, pairs), jnp.int32),
            pltpu.VMEM((1, pairs), jnp.int32),
            pltpu.VMEM((1, pairs), jnp.int32),
            pltpu.SemaphoreType.DMA((functions,)),
            pltpu.SemaphoreType.DMA((6,)),
        ],
        compiler_params=pltpu.CompilerParams(vmem_limit_bytes=8 << 20),
        name="pack",
    )(
        fixed(anchor),
        fixed(support.transpose(1, 2, 0, 3)),
        fixed(kernel.transpose(1, 2, 0)),
        fixed(pair_owner.reshape(1, pairs)),
        fixed(pair_partner.reshape(1, pairs)),
        fixed(pair_live.reshape(1, pairs)),
    )
    own, onward = packed[:ways], packed[ways:]
    upper, peers = [], []
    for k in range(ways):
        upper.append(moved_by(onward[k], ("space", "orb"), (1, k)))
    for k in range(1, ways):
        peers.append(moved_by(own[k], ("orb",), (k,)))
    sources = [own[0]] + peers + upper

    rows = functions * band
    padded = round_up(rows, LANES)
    size = spans_of(functions, pairs, band)[1]
    head = round_up(groups * functions, 8)
    order = [0] + [ways] + list(range(1, ways)) + [ways + k for k in range(1, ways)]
    kept = [
        pltpu.VMEM((padded, planes * points), BF16),
        pltpu.VMEM((rows, 2 * padded), BF16),
        pltpu.VMEM((2 * ways, *size), BF16),
        pltpu.VMEM((2 * ways, atoms, LANES), F32),
    ]
    held = pl.pallas_call(
        functools.partial(first_kernel, dims),
        out_shape=kept,
        in_specs=[vmem],
        out_specs=[vmem] * 4,
        compiler_params=pltpu.CompilerParams(vmem_limit_bytes=8 << 20),
        name="first",
    )(sources[0])
    for c in order[1:-1]:
        held = pl.pallas_call(
            functools.partial(next_kernel, dims, c),
            out_shape=kept,
            in_specs=[vmem] + [vmem] * 4,
            out_specs=[vmem] * 4,
            input_output_aliases={1 + i: i for i in range(4)},
            compiler_params=pltpu.CompilerParams(vmem_limit_bytes=8 << 20),
        )(sources[c], *held)
    parts = pl.pallas_call(
        functools.partial(main_kernel, dims, order[-1]),
        out_shape=[jax.ShapeDtypeStruct((head + round_up(planes, 8), LANES), F32)] * ways
        + [jax.ShapeDtypeStruct((head, LANES), F32)] * ways
        + kept,
        in_specs=[vmem] * 6,
        out_specs=[vmem] * (2 * ways + 4),
        scratch_shapes=[pltpu.VMEM((rows, planes * points), BF16)],
        input_output_aliases={2 + i: 2 * ways + i for i in range(4)},
        compiler_params=pltpu.CompilerParams(vmem_limit_bytes=20 << 20),
        name="main",
    )(v_ext, sources[order[-1]], *held)
    parts = parts[: 2 * ways]

    own_parts, low_parts = parts[:ways], parts[ways:]
    messages, arrived = [own_parts[0]], []
    for k in range(ways):
        arrived.append(moved_by(low_parts[k], ("space", "orb"), (-1, -k)))
    for k in range(1, ways):
        messages.append(moved_by(own_parts[k], ("orb",), (-k,)))
    mine = arrived[0]
    for part in arrived[1:]:
        mine = mine + part
    for message in messages:
        mine = mine + message[:head]
    shares = lax.axis_size("grid")
    other = moved_by(mine, ("grid",), (1,))
    for k in range(2, shares):
        other = other + moved_by(mine, ("grid",), (k,))
    density, blocks = pl.pallas_call(
        functools.partial(final_kernel, dims),
        out_shape=[
            jax.ShapeDtypeStruct((slab, points), F32),
            jax.ShapeDtypeStruct((functions, functions, pairs), F32),
        ],
        in_specs=[vmem] * (2 + ways),
        out_specs=[hbm] * 2,
        scratch_shapes=[
            pltpu.VMEM((slab, points), F32),
            pltpu.VMEM((functions, functions, pairs), F32),
            pltpu.VMEM((functions, functions, LANES), F32),
            pltpu.SemaphoreType.DMA((2,)),
        ],
        compiler_params=pltpu.CompilerParams(vmem_limit_bytes=4 << 20),
        name="final",
    )(mine, other, *messages)
    return (density, blocks.transpose(2, 0, 1))


def solution(mesh):
    placed = (
        P(("shift", "space", "orb"), None, None, "grid"),
        P(("shift", "space", "orb")),
        P(("shift", "space", "orb"), None, None),
        P(("shift", "space", "orb")),
        P(("shift", "space", "orb")),
        P(("shift", "space", "orb")),
        P(("shift", "space"), "grid"),
    )
    step = jax.shard_map(
        on_device,
        mesh=mesh,
        in_specs=placed,
        out_specs=(P(("shift", "space"), "grid"), P(("shift", "space", "orb"), None, None)),
        check_vma=False,
    )
    ways = mesh.shape["orb"]
    last = source_ref.shape[0] - 1
    for h in range(planes):
        for s in range(functions):
            place = (pl.ds((s * sources + c) * atoms, atoms), pl.ds(h * points, points))
            if h < last:
                f_ref[place] = source_ref[h * block + s * atoms : h * block + (s + 1) * atoms, :]
            else:
                f_ref[place] = jnp.zeros((atoms, points), BF16)
    row_id = lax.broadcasted_iota(jnp.int32, size, 0)
    lane_id = lax.broadcasted_iota(jnp.int32, (1, size[1]), 1)
    function_id = jnp.zeros((1, size[1]), jnp.int32)
    for t in range(1, size[1] // pairs):
        function_id = function_id + (lane_id >= t * pairs).astype(jnp.int32)
    atom_id = lax.broadcasted_iota(jnp.int32, (atoms, LANES), 0)
    base = groups * functions
    pair_high = source_ref[last, 0:height, :].astype(F32)
    pair_low = source_ref[last, height : 2 * height, :].astype(F32)
    owner = pair_high[base : base + 1, :].astype(jnp.int32)
    live = pair_high[base + 1 : base + 2, :]
    code = pair_high[base + 2 : base + 3, :].astype(jnp.int32)
    domain = (code >= per_domain).astype(jnp.int32) + (code >= 2 * per_domain).astype(jnp.int32)
    inside = code - domain * per_domain
    orb_of = jnp.zeros(code.shape, jnp.int32)
    for i in range(1, ways):
        orb_of = orb_of + (inside >= i * atoms).astype(jnp.int32)
    local = inside - orb_of * atoms
    slot = orb - orb_of
    slot = jnp.where(slot < 0, slot + ways, slot)
    if c < ways:
        slot = slot + jnp.where(domain == 0, ways, 0)
        valid = domain <= 1
    else:
        slot = slot + jnp.where(domain == 1, ways, 0)
        valid = domain >= 1
    inner = jnp.where(valid, slot * atoms + local, -padded * LANES)
    inner = jnp.concatenate([inner] * (size[1] // LANES), axis=1)
    target = inner + function_id * band
    table_ref[c] = jnp.where(row_id == target, 1.0, 0.0).astype(BF16)
    own = jnp.where(atom_id == owner, live, 0.0)
    own_ref[c] = own
    for first, count, lanes in spans:
        parts = []
        for pair_rows in (pair_high, pair_low):
            for s in range(functions):
                parts.append(
                    jnp.concatenate(
                        [
                            lined(pair_rows, places[g * per, s], pairs) * own
                            for g in range(first // per, first // per + lanes // LANES)
                        ],
                        axis=1,
                    )
                )
        left = jnp.concatenate(parts, axis=0).astype(BF16)
        cols = count * band
        part = lax.dot_general(
            left, table_ref[c, :cols, :lanes], contract, preferred_element_type=F32
        )
        part = part[:block] + part[block:]
        high = part.astype(BF16)
        low = (part - high.astype(F32)).astype(BF16)
        for s in range(functions):
            place = pl.ds((s * sources + c) * atoms, atoms)
            d_ref[place, first * band : first * band + cols] = high[s * atoms : (s + 1) * atoms]
            d_ref[place, padded + first * band : padded + first * band + cols] = low[
                s * atoms : (s + 1) * atoms
            ]


def first_kernel(dims, source_ref, f_ref, d_ref, table_ref, own_ref):
    rows, padded = d_ref.shape[0], f_ref.shape[0]
    if padded > rows:
        f_ref[rows:, :] = jnp.zeros((padded - rows, f_ref.shape[1]), BF16)
    tail = rows // LANES * LANES
    if padded > tail:
        d_ref[:, tail:padded] = jnp.zeros((rows, padded - tail), BF16)
        d_ref[:, padded + tail :] = jnp.zeros((rows, padded - tail), BF16)
    fill_source(dims, 0, source_ref, f_ref, d_ref, table_ref, own_ref)


def next_kernel(dims, c, source_ref, *rest):
    fill_source(dims, c, source_ref, *rest[4:])


def main_kernel(dims, c, v_ref, source_ref, *rest):
    atoms, functions, _, points, slab, ways, _, pairs, _ = dims
    planes = slab // ways
    sources = 2 * ways
    rest = rest[4:]
    own_outs, low_outs = rest[:ways], rest[ways : 2 * ways]
    f_ref, d_ref, table_ref, own_ref, w_ref = rest[2 * ways :]
    block = functions * atoms
    band = sources * atoms
    rows = functions * band
    per = LANES // pairs
    groups = -(-functions // per)
    spans, _ = spans_of(functions, pairs, band)
    orb = lax.axis_index("orb")
    contract = (((1,), (1,)), ((), ()))
    fill_source(dims, c, source_ref, f_ref, d_ref, table_ref, own_ref)
    f_all = f_ref[...]
    aux = jnp.dot(d_ref[...], jnp.concatenate([f_all, f_all], axis=0), preferred_element_type=F32)
    density = jnp.sum(aux * f_ref[:rows, :].astype(F32), axis=0, keepdims=True)
    v_ext = jnp.concatenate([v_ref[pl.ds(h * ways + orb, 1), :] for h in range(planes)], axis=1)
    potential = v_ext + density / jnp.sqrt(1.0 + density * density)
    w_ref[...] = (f_ref[:rows, :].astype(F32) * potential).astype(BF16)
    blocks = lax.dot_general(w_ref[...], f_ref[:rows, :], contract, preferred_element_type=F32)
    used = groups * functions
    head = round_up(used, 8)
    for out in (*own_outs, *low_outs):
        out[used:, :] = jnp.zeros((out.shape[0] - used, LANES), F32)
    for c in range(sources):
        own = own_ref[c]
        mine = jnp.concatenate(
            [blocks[(s * sources + c) * atoms : (s * sources + c + 1) * atoms] for s in range(functions)],
            axis=0,
        )
        high = mine.astype(BF16)
        low = (mine - high.astype(F32)).astype(BF16)
        both = jnp.concatenate([high, low], axis=0)
        for first, count, lanes in spans:
            cols = count * band
            spread = jnp.dot(
                both[:, first * band : first * band + cols],
                table_ref[c, :cols, :lanes],
                preferred_element_type=F32,
            )
            spread = spread[:block] + spread[block:]
            owned = jnp.concatenate([own] * (lanes // LANES), axis=1)
            picked = jnp.concatenate(
                [
                    jnp.sum(spread[s * atoms : (s + 1) * atoms] * owned, axis=0, keepdims=True)
                    for s in range(functions)
                ],
                axis=0,
            )
            out = own_outs[c] if c < ways else low_outs[c - ways]
            for i in range(lanes // LANES):
                g = first // per + i
                out[g * functions : (g + 1) * functions, :] = picked[:, i * LANES : (i + 1) * LANES]
        if c < ways:
            for h in range(planes):
                own_outs[c][head + h : head + h + 1, :points] = density[
                    :, h * points : (h + 1) * points
                ]


def final_kernel(dims, mine_ref, other_ref, *rest):
    _, functions, _, points, slab, ways, _, pairs, _ = dims
    planes = slab // ways
    message_refs = rest[:ways]
    density_out, blocks_out, density_ref, blocks_ref, pad_ref, sems = rest[ways:]
    orb = lax.axis_index("orb")
    per = LANES // pairs
    groups = -(-functions // per)
    head = round_up(groups * functions, 8)
    for k in range(ways):
        residue = lax.rem(orb + k, ways)
        for h in range(planes):
            density_ref[pl.ds(h * ways + residue, 1), :] = message_refs[k][
                head + h : head + h + 1, :points
            ]
    first = pltpu.make_async_copy(density_ref, density_out, sems.at[0])
    first.start()
    total = mine_ref[...] + other_ref[...]
    for t in range(functions):
        g, i = t // per, t % per
        piece = total[g * functions : (g + 1) * functions]
        if i:
            piece = pltpu.roll(piece, LANES - i * pairs, 1)
        pad_ref[t] = piece
    for t in range(functions):
        for s in range(functions):
            blocks_ref[s, t : t + 1, :] = pad_ref[t, s : s + 1, :pairs]
    second = pltpu.make_async_copy(blocks_ref, blocks_out, sems.at[1])
    second.start()
    first.wait()
    second.wait()


def on_device(support, anchor, kernel, pair_owner, pair_partner, pair_live, v_ext):
    atoms, functions, depth, points = support.shape
    pairs = kernel.shape[0]
    slab = v_ext.shape[0]
    ways = lax.axis_size("orb")
    space = lax.axis_size("space")
    planes = slab // ways
    reach = min((depth - 2) // ways + 1, planes)
    dims = (atoms, functions, depth, points, slab, ways, reach, pairs, space)
    block = functions * atoms
    band = 2 * ways * atoms
    per = LANES // pairs
    groups = -(-functions // per)
    height = pieces_of(functions, pairs)[1]
    vmem = pl.BlockSpec(memory_space=pltpu.VMEM)
    hbm = pl.BlockSpec(memory_space=pltpu.HBM)

    packed = pl.pallas_call(
        functools.partial(pack_kernel, dims),
        out_shape=[jax.ShapeDtypeStruct((planes * block + 2 * height, points), BF16)] * ways
        + [jax.ShapeDtypeStruct((reach * block + 2 * height, points), BF16)] * ways,
        in_specs=[hbm] * 6,
        out_specs=[vmem] * (2 * ways),
        scratch_shapes=[
            pltpu.VMEM((functions + 1, 16, LANES), F32),
            pltpu.VMEM((height, LANES), F32),
            pltpu.SMEM((atoms,), jnp.int32),
            pltpu.VMEM((depth, block, points), BF16),
            pltpu.VMEM((functions, functions, pairs), F32),
            pltpu.VMEM((1, pairs), jnp.int32),
            pltpu.VMEM((1, pairs), jnp.int32),
            pltpu.VMEM((1, pairs), jnp.int32),
            pltpu.SemaphoreType.DMA((functions,)),
            pltpu.SemaphoreType.DMA((6,)),
        ],
        compiler_params=pltpu.CompilerParams(vmem_limit_bytes=8 << 20),
        name="pack",
    )(
        fixed(anchor),
        fixed(support.transpose(1, 2, 0, 3)),
        fixed(kernel.transpose(1, 2, 0)),
        fixed(pair_owner.reshape(1, pairs)),
        fixed(pair_partner.reshape(1, pairs)),
        fixed(pair_live.reshape(1, pairs)),
    )
    own, onward = packed[:ways], packed[ways:]
    upper, peers = [], []
    for k in range(ways):
        upper.append(moved_by(onward[k], ("space", "orb"), (1, k)))
    for k in range(1, ways):
        peers.append(moved_by(own[k], ("orb",), (k,)))
    sources = [own[0]] + peers + upper

    rows = functions * band
    padded = round_up(rows, LANES)
    size = spans_of(functions, pairs, band)[1]
    head = round_up(groups * functions, 8)
    order = [0] + [ways] + list(range(1, ways)) + [ways + k for k in range(1, ways)]
    kept = [
        pltpu.VMEM((padded, planes * points), BF16),
        pltpu.VMEM((rows, 2 * padded), BF16),
        pltpu.VMEM((2 * ways, *size), BF16),
        pltpu.VMEM((2 * ways, atoms, LANES), F32),
    ]
    held = pl.pallas_call(
        functools.partial(first_kernel, dims),
        out_shape=kept,
        in_specs=[vmem],
        out_specs=[vmem] * 4,
        compiler_params=pltpu.CompilerParams(vmem_limit_bytes=8 << 20),
        name="first",
    )(sources[0])
    for c in order[1:-1]:
        held = pl.pallas_call(
            functools.partial(next_kernel, dims, c),
            out_shape=kept,
            in_specs=[vmem] + [vmem] * 4,
            out_specs=[vmem] * 4,
            input_output_aliases={1 + i: i for i in range(4)},
            compiler_params=pltpu.CompilerParams(vmem_limit_bytes=8 << 20),
        )(sources[c], *held)
    parts = pl.pallas_call(
        functools.partial(main_kernel, dims, order[-1]),
        out_shape=[jax.ShapeDtypeStruct((head + round_up(planes, 8), LANES), F32)] * ways
        + [jax.ShapeDtypeStruct((head, LANES), F32)] * ways
        + kept,
        in_specs=[vmem] * 6,
        out_specs=[vmem] * (2 * ways + 4),
        scratch_shapes=[pltpu.VMEM((rows, planes * points), BF16)],
        input_output_aliases={2 + i: 2 * ways + i for i in range(4)},
        compiler_params=pltpu.CompilerParams(vmem_limit_bytes=20 << 20),
        name="main",
    )(v_ext, sources[order[-1]], *held)
    parts = parts[: 2 * ways]

    own_parts, low_parts = parts[:ways], parts[ways:]
    messages, arrived = [own_parts[0]], []
    for k in range(ways):
        arrived.append(moved_by(low_parts[k], ("space", "orb"), (-1, -k)))
    for k in range(1, ways):
        messages.append(moved_by(own_parts[k], ("orb",), (-k,)))
    mine = arrived[0]
    for part in arrived[1:]:
        mine = mine + part
    for message in messages:
        mine = mine + message[:head]
    shares = lax.axis_size("grid")
    other = moved_by(mine, ("grid",), (1,))
    for k in range(2, shares):
        other = other + moved_by(mine, ("grid",), (k,))
    density, blocks = pl.pallas_call(
        functools.partial(final_kernel, dims),
        out_shape=[
            jax.ShapeDtypeStruct((slab, points), F32),
            jax.ShapeDtypeStruct((functions, functions, pairs), F32),
        ],
        in_specs=[vmem] * (2 + ways),
        out_specs=[hbm] * 2,
        scratch_shapes=[
            pltpu.VMEM((slab, points), F32),
            pltpu.VMEM((functions, functions, pairs), F32),
            pltpu.VMEM((functions, functions, LANES), F32),
            pltpu.SemaphoreType.DMA((2,)),
        ],
        compiler_params=pltpu.CompilerParams(vmem_limit_bytes=4 << 20),
        name="final",
    )(mine, other, *messages)
    return (density, blocks.transpose(2, 0, 1))


def solution(mesh):
    placed = (
        P(("shift", "space", "orb"), None, None, "grid"),
        P(("shift", "space", "orb")),
        P(("shift", "space", "orb"), None, None),
        P(("shift", "space", "orb")),
        P(("shift", "space", "orb")),
        P(("shift", "space", "orb")),
        P(("shift", "space"), "grid"),
    )
    return jax.shard_map(
        on_device,
        mesh=mesh,
        in_specs=placed,
        out_specs=(P(("shift", "space"), "grid"), P(("shift", "space", "orb"), None, None)),
        check_vma=False,
    )
```

```python
import functools

import jax
import jax.numpy as jnp
from jax import lax
from jax.experimental import pallas as pl
from jax.experimental.pallas import tpu as pltpu
from jax.sharding import PartitionSpec as P


LANES = 128
F32 = jnp.float32
BF16 = jnp.bfloat16


def moved_by(value, axes, steps):
    sizes = [lax.axis_size(axis) for axis in axes]
    pairs = []
    total = 1
    for size in sizes:
        total *= size
    for source in range(total):
        rest, place = source, []
        for size in reversed(sizes):
            place.insert(0, rest % size)
            rest //= size
        target = 0
        for size, here, step in zip(sizes, place, steps):
            target = target * size + (here + step) % size
        pairs.append((source, target))
    return lax.ppermute(value, axes if len(axes) > 1 else axes[0], pairs)


def round_up(count, unit):
    return (count + unit - 1) // unit * unit


def fixed(value):
    return pltpu.with_memory_space_constraint(value, pltpu.HBM)


def pieces_of(functions, pairs):
    per = LANES // pairs
    full = functions // per * per
    places = {}
    for t in range(full):
        for s in range(functions):
            places[t, s] = (t // per * functions + s, t % per)
    count = full * functions
    for t in range(full, functions):
        for s in range(functions):
            places[t, s] = (count // per, count % per)
            count += 1
    for name in range(3):
        places[name] = (count // per, count % per)
        count += 1
    return places, round_up(-(-count // per), 8)


def plane_masks(atoms, points, slab, ways, repeat, anchor_ref, residues):
    rows = atoms * repeat
    row = lax.broadcasted_iota(jnp.int32, (rows, points), 0)
    offset = jnp.zeros((rows, points), jnp.int32)
    for a in range(atoms):
        here = row == a
        for i in range(1, repeat):
            here = here | (row == a + i * atoms)
        offset = jnp.where(here, lax.rem(anchor_ref[a], slab), offset)
    planes = slab // ways
    found = []
    for residue in residues:
        start = offset - residue
        shift = jnp.zeros((rows, points), jnp.int32)
        for low in range(planes):
            shift = shift + (start > low * ways).astype(jnp.int32)
        phase = (shift * ways - start).astype(F32).astype(BF16)
        bits, size = [], 1
        while size <= planes:
            if size % planes:
                bit = ((shift & size) != 0).astype(F32).astype(BF16)
                bits.append((size, bit > 0.5))
            size *= 2
        level = shift.astype(F32).astype(BF16)
        found.append(
            (
                [phase == float(e) for e in range(ways - 1)],
                bits,
                [level <= float(h) for h in range(planes)],
            )
        )
    return found


def early_of(planes):
    return max(1, planes * 3 // 8)


def pack_kernel(dims, *rest):
    atoms, functions, depth, points, slab, ways, reach, pairs, space = dims
    given, rest = rest[:6], rest[6:]
    own_refs, next_refs, tail_ref = rest[:ways], rest[ways : 2 * ways], rest[2 * ways]
    k_pad, row_pad, *held, x_sem, sems = rest[2 * ways + 1 :]
    early = early_of(slab // ways)
    anchor_ref, x_ref, k_ref, owner_ref, partner_ref, live_ref = held
    block = functions * atoms
    copies = [
        pltpu.make_async_copy(given[i], held[i], sems.at[i]) for i in range(6) if i != 1
    ]
    x_copies = [
        pltpu.make_async_copy(
            given[1].at[s], x_ref.at[:, pl.ds(s * atoms, atoms), :], x_sem.at[s]
        )
        for s in range(functions)
    ]
    copies[0].start()
    for copy in x_copies:
        copy.start()
    for copy in copies[1:]:
        copy.start()
    k_pad[...] = jnp.zeros_like(k_pad)
    row_pad[...] = jnp.zeros_like(row_pad)
    planes = slab // ways
    orb, domain = lax.axis_index("orb"), lax.axis_index("space")
    copies[0].wait()
    residues = [lax.rem(orb + k, ways) for k in range(ways)]
    first = 0
    masks = {}
    while first < functions:
        repeat = min(2, functions - first)
        if repeat not in masks:
            masks[repeat] = plane_masks(atoms, points, slab, ways, repeat, anchor_ref, residues)
        for s in range(first, first + repeat):
            x_copies[s].wait()
        rows = atoms * repeat
        zero = jnp.zeros((rows, points), BF16)
        tiles = [x_ref[j, first * atoms : first * atoms + rows, :] for j in range(depth)]
        tiles = tiles + [zero] * (planes * ways - depth)
        for k in range(ways):
            phases, bits, levels = masks[repeat][k]
            line = []
            for m in range(planes):
                pick = tiles[m * ways + ways - 1]
                for e in reversed(range(ways - 1)):
                    pick = jnp.where(phases[e], tiles[m * ways + e], pick)
                line.append(pick)
            for size, mask in bits:
                line = [jnp.where(mask, line[(h - size) % planes], line[h]) for h in range(planes)]
            for h in range(planes):
                place = h * block + first * atoms
                own_refs[k][place : place + rows, :] = jnp.where(levels[h], line[h], zero)
                if h < reach:
                    out, base = next_refs[k], place
                    if k == ways - 1 and h >= early:
                        out, base = tail_ref, place - early * block
                    out[base : base + rows, :] = jnp.where(levels[h], zero, line[h])
        first += repeat
    for copy in copies[1:]:
        copy.wait()
    places, height = pieces_of(functions, pairs)
    k_pad[0:functions, :functions, :pairs] = k_ref[...]
    per_domain = atoms * ways
    owner = owner_ref[...] - (domain * ways + orb) * atoms
    partner = partner_ref[...]
    home = jnp.floor((partner.astype(F32) + 0.5) * (1.0 / per_domain)).astype(jnp.int32)
    relative = home - domain + 1
    relative = jnp.where(relative < 0, relative + space, relative)
    relative = jnp.where(relative >= space, relative - space, relative)
    code = relative * per_domain + partner - home * per_domain
    k_pad[functions, 0:1, :pairs] = owner.astype(F32)
    k_pad[functions, 1:2, :pairs] = live_ref[...].astype(F32)
    k_pad[functions, 2:3, :pairs] = code.astype(F32)
    lines = {}
    for name, (row, column) in places.items():
        if isinstance(name, tuple):
            piece = k_pad[name[1], name[0] : name[0] + 1, :]
        else:
            piece = k_pad[functions, name : name + 1, :]
        piece = pltpu.roll(piece, column * pairs, 1) if column else piece
        lines[row] = lines[row] + piece if row in lines else piece
    for row, line in lines.items():
        row_pad[row : row + 1, :] = line
    info = row_pad[...]
    high = info.astype(BF16)
    low = (info - high.astype(F32)).astype(BF16)
    for ref in (*own_refs, *next_refs):
        last = ref.shape[0] - 2 * height
        ref[last : last + height, :] = high
        ref[last + height :, :] = low


def spans_of(functions, pairs, band):
    most = 256 // max(band, pairs)
    spans, first = [], 0
    while first < functions:
        count = min(most, functions - first)
        spans.append((first, count, round_up(count * pairs, LANES)))
        first += count
    return spans, (most * band, round_up(most * pairs, LANES))


def lined(rows, place, pairs):
    row, column = place
    line = rows[row : row + 1, :]
    return pltpu.roll(line, LANES - column * pairs, 1) if column else line


def fill_source(dims, c, source_ref, f_ref, d_ref, table_ref, own_ref):
    atoms, functions, _, points, slab, ways, _, pairs, _ = dims
    orb = lax.axis_index("orb")
    planes = slab // ways
    sources = 2 * ways
    block = functions * atoms
    band = sources * atoms
    padded = f_ref.shape[0]
    per = LANES // pairs
    places, height = pieces_of(functions, pairs)
    spans, size = spans_of(functions, pairs, band)
    per_domain = atoms * ways
    contract = (((1,), (1,)), ((), ()))
    last = (source_ref.shape[0] - 2 * height) // block
    for h in range(early_of(planes) if c == 2 * ways - 1 else planes):
        for s in range(functions):
            place = (pl.ds((s * sources + c) * atoms, atoms), pl.ds(h * points, points))
            if h < last:
                f_ref[place] = source_ref[h * block + s * atoms : h * block + (s + 1) * atoms, :]
            else:
                f_ref[place] = jnp.zeros((atoms, points), BF16)
    row_id = lax.broadcasted_iota(jnp.int32, size, 0)
    lane_id = lax.broadcasted_iota(jnp.int32, (1, size[1]), 1)
    function_id = jnp.zeros((1, size[1]), jnp.int32)
    for t in range(1, size[1] // pairs):
        function_id = function_id + (lane_id >= t * pairs).astype(jnp.int32)
    atom_id = lax.broadcasted_iota(jnp.int32, (atoms, LANES), 0)
    pair_high = source_ref[last * block : last * block + height, :].astype(F32)
    pair_low = source_ref[last * block + height : last * block + 2 * height, :].astype(F32)
    row_lane = lax.broadcasted_iota(jnp.int32, (1, LANES), 1)
    wide = []
    for name in range(3):
        row, column = places[name]
        piece = pair_high[row : row + 1, :]
        piece = jnp.where(
            (row_lane >= column * pairs) & (row_lane < (column + 1) * pairs), piece, 0.0
        )
        line = piece
        for i in range(1, per):
            line = line + pltpu.roll(piece, i * pairs, 1)
        wide.append(line)
    owner, live, code = wide[0].astype(jnp.int32), wide[1], wide[2].astype(jnp.int32)
    domain = (code >= per_domain).astype(jnp.int32) + (code >= 2 * per_domain).astype(jnp.int32)
    inside = code - domain * per_domain
    orb_of = jnp.zeros(code.shape, jnp.int32)
    for i in range(1, ways):
        orb_of = orb_of + (inside >= i * atoms).astype(jnp.int32)
    local = inside - orb_of * atoms
    slot = orb - orb_of
    slot = jnp.where(slot < 0, slot + ways, slot)
    if c < ways:
        slot = slot + jnp.where(domain == 0, ways, 0)
        valid = domain <= 1
    else:
        slot = slot + jnp.where(domain == 1, ways, 0)
        valid = domain >= 1
    inner = jnp.where(valid, slot * atoms + local, -padded * LANES)
    inner = jnp.concatenate([inner] * (size[1] // LANES), axis=1)
    target = inner + function_id * band
    table_ref[c] = jnp.where(row_id == target, 1.0, 0.0).astype(BF16)
    own = jnp.where(atom_id == owner, live, 0.0)
    own_ref[c] = own
    for first, count, lanes in spans:
        parts = []
        for pair_rows in (pair_high, pair_low):
            for s in range(functions):
                parts.append(
                    jnp.concatenate(
                        [
                            lined(pair_rows, places[g * per, s], pairs) * own
                            for g in range(first // per, first // per + lanes // LANES)
                        ],
                        axis=1,
                    )
                )
        left = jnp.concatenate(parts, axis=0).astype(BF16)
        cols = count * band
        whole = functions * band // 256 * 256
        if first * band < whole:
            at, next_at = first * band, whole + first * band
        else:
            at = whole + first * band
            next_at = at + functions * band - whole
        part = lax.dot_general(
            left, table_ref[c, :cols, :lanes], contract, preferred_element_type=F32
        )
        part = part[:block] + part[block:]
        high = part.astype(BF16)
        low = (part - high.astype(F32)).astype(BF16)
        for s in range(functions):
            place = pl.ds((s * sources + c) * atoms, atoms)
            d_ref[place, at : at + cols] = high[s * atoms : (s + 1) * atoms]
            d_ref[place, next_at : next_at + cols] = low[s * atoms : (s + 1) * atoms]


def first_kernel(dims, source_ref, f_ref, d_ref, table_ref, own_ref):
    rows, width = d_ref.shape
    if width > 2 * rows:
        edge = 2 * rows // LANES * LANES
        d_ref[:, edge:] = jnp.zeros((rows, width - edge), BF16)
    fill_source(dims, 0, source_ref, f_ref, d_ref, table_ref, own_ref)


def next_kernel(dims, c, source_ref, *rest):
    fill_source(dims, c, source_ref, *rest[4:])


def main_kernel(dims, c, v_ref, tail_ref, d_ref, table_ref, own_ref, *rest):
    atoms, functions, _, points, slab, ways, reach, pairs, _ = dims
    planes = slab // ways
    sources = 2 * ways
    rest = rest[1:]
    own_outs, low_outs = rest[:ways], rest[ways : 2 * ways]
    f_ref, w_ref = rest[2 * ways :]
    block = functions * atoms
    band = sources * atoms
    rows = functions * band
    per = LANES // pairs
    groups = -(-functions // per)
    spans, _ = spans_of(functions, pairs, band)
    orb = lax.axis_index("orb")
    contract = (((1,), (1,)), ((), ()))
    early = early_of(planes)
    for h in range(early, planes):
        for s in range(functions):
            place = (pl.ds((s * sources + c) * atoms, atoms), pl.ds(h * points, points))
            if h < reach:
                at = (h - early) * block + s * atoms
                f_ref[place] = tail_ref[at : at + atoms, :]
            else:
                f_ref[place] = jnp.zeros((atoms, points), BF16)
    whole = rows // 256 * 256
    body, rest_rows = f_ref[:whole, :], f_ref[whole:rows, :]
    stacked = [body, body, rest_rows, rest_rows]
    if d_ref.shape[1] > 2 * rows:
        stacked.append(jnp.zeros((d_ref.shape[1] - 2 * rows, planes * points), BF16))
    aux = jnp.dot(d_ref[...], jnp.concatenate(stacked, axis=0), preferred_element_type=F32)
    density = jnp.sum(aux * f_ref[:rows, :].astype(F32), axis=0, keepdims=True)
    v_ext = jnp.concatenate([v_ref[pl.ds(h * ways + orb, 1), :] for h in range(planes)], axis=1)
    potential = v_ext + density / jnp.sqrt(1.0 + density * density)
    w_ref[...] = (f_ref[:rows, :].astype(F32) * potential).astype(BF16)
    blocks = lax.dot_general(w_ref[...], f_ref[:rows, :], contract, preferred_element_type=F32)
    used = groups * functions
    head = round_up(used, 8)
    for out in (*own_outs, *low_outs):
        out[used:, :] = jnp.zeros((out.shape[0] - used, LANES), F32)
    for c in range(sources):
        own = own_ref[c]
        mine = jnp.concatenate(
            [blocks[(s * sources + c) * atoms : (s * sources + c + 1) * atoms] for s in range(functions)],
            axis=0,
        )
        high = mine.astype(BF16)
        low = (mine - high.astype(F32)).astype(BF16)
        both = jnp.concatenate([high, low], axis=0)
        for first, count, lanes in spans:
            cols = count * band
            spread = jnp.dot(
                both[:, first * band : first * band + cols],
                table_ref[c, :cols, :lanes],
                preferred_element_type=F32,
            )
            spread = spread[:block] + spread[block:]
            owned = jnp.concatenate([own] * (lanes // LANES), axis=1)
            picked = jnp.concatenate(
                [
                    jnp.sum(spread[s * atoms : (s + 1) * atoms] * owned, axis=0, keepdims=True)
                    for s in range(functions)
                ],
                axis=0,
            )
            out = own_outs[c] if c < ways else low_outs[c - ways]
            for i in range(lanes // LANES):
                g = first // per + i
                out[g * functions : (g + 1) * functions, :] = picked[:, i * LANES : (i + 1) * LANES]
        if c < ways:
            for h in range(planes):
                own_outs[c][head + h : head + h + 1, :points] = density[
                    :, h * points : (h + 1) * points
                ]


def final_kernel(dims, mine_ref, other_ref, *rest):
    _, functions, _, points, slab, ways, _, pairs, _ = dims
    planes = slab // ways
    message_refs = rest[:ways]
    density_out, blocks_out, density_ref, blocks_ref, pad_ref, sems = rest[ways:]
    orb = lax.axis_index("orb")
    per = LANES // pairs
    groups = -(-functions // per)
    head = round_up(groups * functions, 8)
    for k in range(ways):
        residue = lax.rem(orb + k, ways)
        for h in range(planes):
            density_ref[pl.ds(h * ways + residue, 1), :] = message_refs[k][
                head + h : head + h + 1, :points
            ]
    first = pltpu.make_async_copy(density_ref, density_out, sems.at[0])
    first.start()
    total = mine_ref[...] + other_ref[...]
    for t in range(functions):
        g, i = t // per, t % per
        piece = total[g * functions : (g + 1) * functions]
        if i:
            piece = pltpu.roll(piece, LANES - i * pairs, 1)
        pad_ref[t] = piece
    for t in range(functions):
        for s in range(functions):
            blocks_ref[s, t : t + 1, :] = pad_ref[t, s : s + 1, :pairs]
    second = pltpu.make_async_copy(blocks_ref, blocks_out, sems.at[1])
    second.start()
    first.wait()
    second.wait()


def on_device(support, anchor, kernel, pair_owner, pair_partner, pair_live, v_ext):
    atoms, functions, depth, points = support.shape
    pairs = kernel.shape[0]
    slab = v_ext.shape[0]
    ways = lax.axis_size("orb")
    space = lax.axis_size("space")
    planes = slab // ways
    reach = min((depth - 2) // ways + 1, planes)
    early = early_of(planes)
    dims = (atoms, functions, depth, points, slab, ways, reach, pairs, space)
    block = functions * atoms
    band = 2 * ways * atoms
    per = LANES // pairs
    groups = -(-functions // per)
    height = pieces_of(functions, pairs)[1]
    vmem = pl.BlockSpec(memory_space=pltpu.VMEM)
    hbm = pl.BlockSpec(memory_space=pltpu.HBM)

    packed = pl.pallas_call(
        functools.partial(pack_kernel, dims),
        out_shape=[jax.ShapeDtypeStruct((planes * block + 2 * height, points), BF16)] * ways
        + [jax.ShapeDtypeStruct((reach * block + 2 * height, points), BF16)] * (ways - 1)
        + [
            jax.ShapeDtypeStruct((early * block + 2 * height, points), BF16),
            jax.ShapeDtypeStruct(((reach - early) * block, points), BF16),
        ],
        in_specs=[hbm] * 6,
        out_specs=[vmem] * (2 * ways + 1),
        scratch_shapes=[
            pltpu.VMEM((functions + 1, 16, LANES), F32),
            pltpu.VMEM((height, LANES), F32),
            pltpu.SMEM((atoms,), jnp.int32),
            pltpu.VMEM((depth, block, points), BF16),
            pltpu.VMEM((functions, functions, pairs), F32),
            pltpu.VMEM((1, pairs), jnp.int32),
            pltpu.VMEM((1, pairs), jnp.int32),
            pltpu.VMEM((1, pairs), jnp.int32),
            pltpu.SemaphoreType.DMA((functions,)),
            pltpu.SemaphoreType.DMA((6,)),
        ],
        compiler_params=pltpu.CompilerParams(vmem_limit_bytes=8 << 20),
        name="pack",
    )(
        fixed(anchor),
        fixed(support.transpose(1, 2, 0, 3)),
        fixed(kernel.transpose(1, 2, 0)),
        fixed(pair_owner.reshape(1, pairs)),
        fixed(pair_partner.reshape(1, pairs)),
        fixed(pair_live.reshape(1, pairs)),
    )
    own, onward, tail = packed[:ways], packed[ways : 2 * ways], packed[2 * ways]
    upper, peers = [], []
    for k in range(ways):
        upper.append(moved_by(onward[k], ("space", "orb"), (1, k)))
    for k in range(1, ways):
        peers.append(moved_by(own[k], ("orb",), (k,)))
    tail = moved_by(tail, ("space", "orb"), (1, ways - 1))
    sources = [own[0]] + peers + upper

    rows = functions * band
    size = spans_of(functions, pairs, band)[1]
    head = round_up(groups * functions, 8)
    order = [0] + [ways] + list(range(1, ways)) + [ways + k for k in range(1, ways)]
    kept = [
        pltpu.VMEM((rows, planes * points), BF16),
        pltpu.VMEM((rows, round_up(2 * rows, LANES)), BF16),
        pltpu.VMEM((2 * ways, *size), BF16),
        pltpu.VMEM((2 * ways, atoms, LANES), F32),
    ]
    held = pl.pallas_call(
        functools.partial(first_kernel, dims),
        out_shape=kept,
        in_specs=[vmem],
        out_specs=[vmem] * 4,
        compiler_params=pltpu.CompilerParams(vmem_limit_bytes=8 << 20),
        name="first",
    )(sources[0])
    for c in order[1:]:
        held = pl.pallas_call(
            functools.partial(next_kernel, dims, c),
            out_shape=kept,
            in_specs=[vmem] + [vmem] * 4,
            out_specs=[vmem] * 4,
            input_output_aliases={1 + i: i for i in range(4)},
            compiler_params=pltpu.CompilerParams(vmem_limit_bytes=8 << 20),
        )(sources[c], *held)
    f_all, d_all, tables, owns = held
    parts = pl.pallas_call(
        functools.partial(main_kernel, dims, order[-1]),
        out_shape=[jax.ShapeDtypeStruct((head + round_up(planes, 8), LANES), F32)] * ways
        + [jax.ShapeDtypeStruct((head, LANES), F32)] * ways
        + kept[:1],
        in_specs=[vmem] * 6,
        out_specs=[vmem] * (2 * ways + 1),
        scratch_shapes=[pltpu.VMEM((rows, planes * points), BF16)],
        input_output_aliases={5: 2 * ways},
        compiler_params=pltpu.CompilerParams(vmem_limit_bytes=20 << 20),
        name="main",
    )(v_ext, tail, d_all, tables, owns, f_all)
    parts = parts[: 2 * ways]

    own_parts, low_parts = parts[:ways], parts[ways:]
    messages, arrived = [own_parts[0]], []
    for k in range(ways):
        arrived.append(moved_by(low_parts[k], ("space", "orb"), (-1, -k)))
    for k in range(1, ways):
        messages.append(moved_by(own_parts[k], ("orb",), (-k,)))
    mine = arrived[0]
    for part in arrived[1:]:
        mine = mine + part
    for message in messages:
        mine = mine + message[:head]
    shares = lax.axis_size("grid")
    other = moved_by(mine, ("grid",), (1,))
    for k in range(2, shares):
        other = other + moved_by(mine, ("grid",), (k,))
    density, blocks = pl.pallas_call(
        functools.partial(final_kernel, dims),
        out_shape=[
            jax.ShapeDtypeStruct((slab, points), F32),
            jax.ShapeDtypeStruct((functions, functions, pairs), F32),
        ],
        in_specs=[vmem] * (2 + ways),
        out_specs=[hbm] * 2,
        scratch_shapes=[
            pltpu.VMEM((slab, points), F32),
            pltpu.VMEM((functions, functions, pairs), F32),
            pltpu.VMEM((functions, functions, LANES), F32),
            pltpu.SemaphoreType.DMA((2,)),
        ],
        compiler_params=pltpu.CompilerParams(vmem_limit_bytes=4 << 20),
        name="final",
    )(mine, other, *messages)
    return (density, blocks.transpose(2, 0, 1))


def solution(mesh):
    placed = (
        P(("shift", "space", "orb"), None, None, "grid"),
        P(("shift", "space", "orb")),
        P(("shift", "space", "orb"), None, None),
        P(("shift", "space", "orb")),
        P(("shift", "space", "orb")),
        P(("shift", "space", "orb")),
        P(("shift", "space"), "grid"),
    )
    return jax.shard_map(
        on_device,
        mesh=mesh,
        in_specs=placed,
        out_specs=(P(("shift", "space"), "grid"), P(("shift", "space", "orb"), None, None)),
        check_vma=False,
    )
```

```python
import functools

import jax
import jax.numpy as jnp
from jax import lax
from jax.experimental import pallas as pl
from jax.experimental.pallas import tpu as pltpu
from jax.sharding import PartitionSpec as P


LANES = 128
F32 = jnp.float32
BF16 = jnp.bfloat16


def moved_by(value, axes, steps):
    sizes = [lax.axis_size(axis) for axis in axes]
    pairs = []
    total = 1
    for size in sizes:
        total *= size
    for source in range(total):
        rest, place = source, []
        for size in reversed(sizes):
            place.insert(0, rest % size)
            rest //= size
        target = 0
        for size, here, step in zip(sizes, place, steps):
            target = target * size + (here + step) % size
        pairs.append((source, target))
    return lax.ppermute(value, axes if len(axes) > 1 else axes[0], pairs)


def round_up(count, unit):
    return (count + unit - 1) // unit * unit


def fixed(value):
    return pltpu.with_memory_space_constraint(value, pltpu.HBM)


def pieces_of(functions, pairs):
    per = LANES // pairs
    full = functions // per * per
    places = {}
    for t in range(full):
        for s in range(functions):
            places[t, s] = (t // per * functions + s, t % per)
    count = full * functions
    for t in range(full, functions):
        for s in range(functions):
            places[t, s] = (count // per, count % per)
            count += 1
    for name in range(3):
        places[name] = (count // per, count % per)
        count += 1
    return places, round_up(-(-count // per), 8)


def plane_masks(atoms, points, slab, ways, repeat, anchor_ref, residues):
    rows = atoms * repeat
    row = lax.broadcasted_iota(jnp.int32, (rows, points), 0)
    offset = jnp.zeros((rows, points), jnp.int32)
    for a in range(atoms):
        here = row == a
        for i in range(1, repeat):
            here = here | (row == a + i * atoms)
        offset = jnp.where(here, lax.rem(anchor_ref[a], slab), offset)
    planes = slab // ways
    found = []
    for residue in residues:
        start = offset - residue
        shift = jnp.zeros((rows, points), jnp.int32)
        for low in range(planes):
            shift = shift + (start > low * ways).astype(jnp.int32)
        phase = (shift * ways - start).astype(F32).astype(BF16)
        bits, size = [], 1
        while size <= planes:
            if size % planes:
                bit = ((shift & size) != 0).astype(F32).astype(BF16)
                bits.append((size, bit > 0.5))
            size *= 2
        level = shift.astype(F32).astype(BF16)
        found.append(
            (
                [phase == float(e) for e in range(ways - 1)],
                bits,
                [level <= float(h) for h in range(planes)],
            )
        )
    return found


def early_of(planes):
    return max(1, planes * 2 // 8)


def pack_kernel(dims, *rest):
    atoms, functions, depth, points, slab, ways, reach, pairs, space = dims
    given, rest = rest[:6], rest[6:]
    own_refs, next_refs, tail_ref = rest[:ways], rest[ways : 2 * ways], rest[2 * ways]
    k_pad, row_pad, *held, x_sem, sems = rest[2 * ways + 1 :]
    early = early_of(slab // ways)
    anchor_ref, x_ref, k_ref, owner_ref, partner_ref, live_ref = held
    block = functions * atoms
    copies = [
        pltpu.make_async_copy(given[i], held[i], sems.at[i]) for i in range(6) if i != 1
    ]
    x_copies = [
        pltpu.make_async_copy(
            given[1].at[s], x_ref.at[:, pl.ds(s * atoms, atoms), :], x_sem.at[s]
        )
        for s in range(functions)
    ]
    copies[0].start()
    for copy in x_copies:
        copy.start()
    for copy in copies[1:]:
        copy.start()
    k_pad[...] = jnp.zeros_like(k_pad)
    row_pad[...] = jnp.zeros_like(row_pad)
    planes = slab // ways
    orb, domain = lax.axis_index("orb"), lax.axis_index("space")
    copies[0].wait()
    residues = [lax.rem(orb + k, ways) for k in range(ways)]
    first, waiting = 0, x_copies + copies[1:]
    masks = {}
    while first < functions:
        repeat = min(2, functions - first)
        if repeat not in masks:
            masks[repeat] = plane_masks(atoms, points, slab, ways, repeat, anchor_ref, residues)
        if first + 4 >= functions:
            for copy in waiting:
                copy.wait()
            waiting = []
        else:
            for s in range(first, first + repeat):
                x_copies[s].wait()
            waiting = waiting[repeat:]
        rows = atoms * repeat
        zero = jnp.zeros((rows, points), BF16)
        tiles = [x_ref[j, first * atoms : first * atoms + rows, :] for j in range(depth)]
        tiles = tiles + [zero] * (planes * ways - depth)
        for k in range(ways):
            phases, bits, levels = masks[repeat][k]
            line = []
            for m in range(planes):
                pick = tiles[m * ways + ways - 1]
                for e in reversed(range(ways - 1)):
                    pick = jnp.where(phases[e], tiles[m * ways + e], pick)
                line.append(pick)
            for size, mask in bits:
                line = [jnp.where(mask, line[(h - size) % planes], line[h]) for h in range(planes)]
            for h in range(planes):
                place = h * block + first * atoms
                own_refs[k][place : place + rows, :] = jnp.where(levels[h], line[h], zero)
                if h < reach:
                    out, base = next_refs[k], place
                    if k == ways - 1 and h >= early:
                        out, base = tail_ref, place - early * block
                    out[base : base + rows, :] = jnp.where(levels[h], zero, line[h])
        first += repeat
    places, height = pieces_of(functions, pairs)
    k_pad[0:functions, :functions, :pairs] = k_ref[...]
    per_domain = atoms * ways
    owner = owner_ref[...] - (domain * ways + orb) * atoms
    partner = partner_ref[...]
    home = jnp.floor((partner.astype(F32) + 0.5) * (1.0 / per_domain)).astype(jnp.int32)
    relative = home - domain + 1
    relative = jnp.where(relative < 0, relative + space, relative)
    relative = jnp.where(relative >= space, relative - space, relative)
    code = relative * per_domain + partner - home * per_domain
    k_pad[functions, 0:1, :pairs] = owner.astype(F32)
    k_pad[functions, 1:2, :pairs] = live_ref[...].astype(F32)
    k_pad[functions, 2:3, :pairs] = code.astype(F32)
    lines = {}
    for name, (row, column) in places.items():
        if isinstance(name, tuple):
            piece = k_pad[name[1], name[0] : name[0] + 1, :]
        else:
            piece = k_pad[functions, name : name + 1, :]
        piece = pltpu.roll(piece, column * pairs, 1) if column else piece
        lines[row] = lines[row] + piece if row in lines else piece
    for row, line in lines.items():
        row_pad[row : row + 1, :] = line
    info = row_pad[...]
    high = info.astype(BF16)
    low = (info - high.astype(F32)).astype(BF16)
    for ref in (*own_refs, *next_refs):
        last = ref.shape[0] - 2 * height
        ref[last : last + height, :] = high
        ref[last + height :, :] = low


def spans_of(functions, pairs, band):
    most = 256 // max(band, pairs)
    spans, first = [], 0
    while first < functions:
        count = min(most, functions - first)
        spans.append((first, count, round_up(count * pairs, LANES)))
        first += count
    return spans, (most * band, round_up(most * pairs, LANES))


def lined(rows, place, pairs):
    row, column = place
    line = rows[row : row + 1, :]
    return pltpu.roll(line, LANES - column * pairs, 1) if column else line


def fill_source(dims, c, source_ref, f_ref, d_ref, table_ref, own_ref):
    atoms, functions, _, points, slab, ways, _, pairs, _ = dims
    orb = lax.axis_index("orb")
    planes = slab // ways
    sources = 2 * ways
    block = functions * atoms
    band = sources * atoms
    padded = f_ref.shape[0]
    per = LANES // pairs
    places, height = pieces_of(functions, pairs)
    spans, size = spans_of(functions, pairs, band)
    per_domain = atoms * ways
    contract = (((1,), (1,)), ((), ()))
    last = (source_ref.shape[0] - 2 * height) // block
    for h in range(early_of(planes) if c == 2 * ways - 1 else planes):
        for s in range(functions):
            place = (pl.ds((s * sources + c) * atoms, atoms), pl.ds(h * points, points))
            if h < last:
                f_ref[place] = source_ref[h * block + s * atoms : h * block + (s + 1) * atoms, :]
            else:
                f_ref[place] = jnp.zeros((atoms, points), BF16)
    row_id = lax.broadcasted_iota(jnp.int32, size, 0)
    lane_id = lax.broadcasted_iota(jnp.int32, (1, size[1]), 1)
    function_id = jnp.zeros((1, size[1]), jnp.int32)
    for t in range(1, size[1] // pairs):
        function_id = function_id + (lane_id >= t * pairs).astype(jnp.int32)
    atom_id = lax.broadcasted_iota(jnp.int32, (atoms, LANES), 0)
    pair_high = source_ref[last * block : last * block + height, :].astype(F32)
    pair_low = source_ref[last * block + height : last * block + 2 * height, :].astype(F32)
    row_lane = lax.broadcasted_iota(jnp.int32, (1, LANES), 1)
    wide = []
    for name in range(3):
        row, column = places[name]
        piece = pair_high[row : row + 1, :]
        piece = jnp.where(
            (row_lane >= column * pairs) & (row_lane < (column + 1) * pairs), piece, 0.0
        )
        line = piece
        for i in range(1, per):
            line = line + pltpu.roll(piece, i * pairs, 1)
        wide.append(line)
    owner, live, code = wide[0].astype(jnp.int32), wide[1], wide[2].astype(jnp.int32)
    domain = (code >= per_domain).astype(jnp.int32) + (code >= 2 * per_domain).astype(jnp.int32)
    inside = code - domain * per_domain
    orb_of = jnp.zeros(code.shape, jnp.int32)
    for i in range(1, ways):
        orb_of = orb_of + (inside >= i * atoms).astype(jnp.int32)
    local = inside - orb_of * atoms
    slot = orb - orb_of
    slot = jnp.where(slot < 0, slot + ways, slot)
    if c < ways:
        slot = slot + jnp.where(domain == 0, ways, 0)
        valid = domain <= 1
    else:
        slot = slot + jnp.where(domain == 1, ways, 0)
        valid = domain >= 1
    inner = jnp.where(valid, slot * atoms + local, -padded * LANES)
    inner = jnp.concatenate([inner] * (size[1] // LANES), axis=1)
    target = inner + function_id * band
    table_ref[c] = jnp.where(row_id == target, 1.0, 0.0).astype(BF16)
    own = jnp.where(atom_id == owner, live, 0.0)
    own_ref[c] = own
    for first, count, lanes in spans:
        parts = []
        for pair_rows in (pair_high, pair_low):
            for s in range(functions):
                parts.append(
                    jnp.concatenate(
                        [
                            lined(pair_rows, places[g * per, s], pairs) * own
                            for g in range(first // per, first // per + lanes // LANES)
                        ],
                        axis=1,
                    )
                )
        left = jnp.concatenate(parts, axis=0).astype(BF16)
        cols = count * band
        whole = functions * band // 256 * 256
        if first * band < whole:
            at, next_at = first * band, whole + first * band
        else:
            at = whole + first * band
            next_at = at + functions * band - whole
        part = lax.dot_general(
            left, table_ref[c, :cols, :lanes], contract, preferred_element_type=F32
        )
        part = part[:block] + part[block:]
        high = part.astype(BF16)
        low = (part - high.astype(F32)).astype(BF16)
        for s in range(functions):
            place = pl.ds((s * sources + c) * atoms, atoms)
            d_ref[place, at : at + cols] = high[s * atoms : (s + 1) * atoms]
            d_ref[place, next_at : next_at + cols] = low[s * atoms : (s + 1) * atoms]


def first_kernel(dims, source_ref, f_ref, d_ref, table_ref, own_ref):
    rows, width = d_ref.shape
    if width > 2 * rows:
        edge = 2 * rows // LANES * LANES
        d_ref[:, edge:] = jnp.zeros((rows, width - edge), BF16)
    fill_source(dims, 0, source_ref, f_ref, d_ref, table_ref, own_ref)


def next_kernel(dims, c, source_ref, *rest):
    fill_source(dims, c, source_ref, *rest[4:])


def main_kernel(dims, c, v_ref, tail_ref, d_ref, table_ref, own_ref, *rest):
    atoms, functions, _, points, slab, ways, reach, pairs, _ = dims
    planes = slab // ways
    sources = 2 * ways
    rest = rest[1:]
    own_outs, low_outs = rest[:ways], rest[ways : 2 * ways]
    f_ref, w_ref = rest[2 * ways :]
    block = functions * atoms
    band = sources * atoms
    rows = functions * band
    per = LANES // pairs
    groups = -(-functions // per)
    spans, _ = spans_of(functions, pairs, band)
    orb = lax.axis_index("orb")
    contract = (((1,), (1,)), ((), ()))
    early = early_of(planes)
    for h in range(early, planes):
        for s in range(functions):
            place = (pl.ds((s * sources + c) * atoms, atoms), pl.ds(h * points, points))
            if h < reach:
                at = (h - early) * block + s * atoms
                f_ref[place] = tail_ref[at : at + atoms, :]
            else:
                f_ref[place] = jnp.zeros((atoms, points), BF16)
    whole = rows // 256 * 256
    body, rest_rows = f_ref[:whole, :], f_ref[whole:rows, :]
    stacked = [body, body, rest_rows, rest_rows]
    if d_ref.shape[1] > 2 * rows:
        stacked.append(jnp.zeros((d_ref.shape[1] - 2 * rows, planes * points), BF16))
    aux = jnp.dot(d_ref[...], jnp.concatenate(stacked, axis=0), preferred_element_type=F32)
    density = jnp.sum(aux * f_ref[:rows, :].astype(F32), axis=0, keepdims=True)
    v_ext = jnp.concatenate([v_ref[pl.ds(h * ways + orb, 1), :] for h in range(planes)], axis=1)
    potential = v_ext + density / jnp.sqrt(1.0 + density * density)
    w_ref[...] = (f_ref[:rows, :].astype(F32) * potential).astype(BF16)
    blocks = lax.dot_general(w_ref[...], f_ref[:rows, :], contract, preferred_element_type=F32)
    used = groups * functions
    head = round_up(used, 8)
    for out in (*own_outs, *low_outs):
        out[used:, :] = jnp.zeros((out.shape[0] - used, LANES), F32)
    for c in range(sources):
        own = own_ref[c]
        mine = jnp.concatenate(
            [blocks[(s * sources + c) * atoms : (s * sources + c + 1) * atoms] for s in range(functions)],
            axis=0,
        )
        high = mine.astype(BF16)
        low = (mine - high.astype(F32)).astype(BF16)
        both = jnp.concatenate([high, low], axis=0)
        for first, count, lanes in spans:
            cols = count * band
            spread = jnp.dot(
                both[:, first * band : first * band + cols],
                table_ref[c, :cols, :lanes],
                preferred_element_type=F32,
            )
            spread = spread[:block] + spread[block:]
            owned = jnp.concatenate([own] * (lanes // LANES), axis=1)
            picked = jnp.concatenate(
                [
                    jnp.sum(spread[s * atoms : (s + 1) * atoms] * owned, axis=0, keepdims=True)
                    for s in range(functions)
                ],
                axis=0,
            )
            out = own_outs[c] if c < ways else low_outs[c - ways]
            for i in range(lanes // LANES):
                g = first // per + i
                out[g * functions : (g + 1) * functions, :] = picked[:, i * LANES : (i + 1) * LANES]
        if c < ways:
            for h in range(planes):
                own_outs[c][head + h : head + h + 1, :points] = density[
                    :, h * points : (h + 1) * points
                ]


def final_kernel(dims, mine_ref, other_ref, *rest):
    _, functions, _, points, slab, ways, _, pairs, _ = dims
    planes = slab // ways
    message_refs = rest[:ways]
    density_out, blocks_out, density_ref, blocks_ref, pad_ref, sems = rest[ways:]
    orb = lax.axis_index("orb")
    per = LANES // pairs
    groups = -(-functions // per)
    head = round_up(groups * functions, 8)
    for k in range(ways):
        residue = lax.rem(orb + k, ways)
        for h in range(planes):
            density_ref[pl.ds(h * ways + residue, 1), :] = message_refs[k][
                head + h : head + h + 1, :points
            ]
    first = pltpu.make_async_copy(density_ref, density_out, sems.at[0])
    first.start()
    total = mine_ref[...] + other_ref[...]
    for t in range(functions):
        g, i = t // per, t % per
        piece = total[g * functions : (g + 1) * functions]
        if i:
            piece = pltpu.roll(piece, LANES - i * pairs, 1)
        pad_ref[t] = piece
    for t in range(functions):
        for s in range(functions):
            blocks_ref[s, t : t + 1, :] = pad_ref[t, s : s + 1, :pairs]
    second = pltpu.make_async_copy(blocks_ref, blocks_out, sems.at[1])
    second.start()
    first.wait()
    second.wait()


def on_device(support, anchor, kernel, pair_owner, pair_partner, pair_live, v_ext):
    atoms, functions, depth, points = support.shape
    pairs = kernel.shape[0]
    slab = v_ext.shape[0]
    ways = lax.axis_size("orb")
    space = lax.axis_size("space")
    planes = slab // ways
    reach = min((depth - 2) // ways + 1, planes)
    early = early_of(planes)
    dims = (atoms, functions, depth, points, slab, ways, reach, pairs, space)
    block = functions * atoms
    band = 2 * ways * atoms
    per = LANES // pairs
    groups = -(-functions // per)
    height = pieces_of(functions, pairs)[1]
    vmem = pl.BlockSpec(memory_space=pltpu.VMEM)
    hbm = pl.BlockSpec(memory_space=pltpu.HBM)

    packed = pl.pallas_call(
        functools.partial(pack_kernel, dims),
        out_shape=[jax.ShapeDtypeStruct((planes * block + 2 * height, points), BF16)] * ways
        + [jax.ShapeDtypeStruct((reach * block + 2 * height, points), BF16)] * (ways - 1)
        + [
            jax.ShapeDtypeStruct((early * block + 2 * height, points), BF16),
            jax.ShapeDtypeStruct(((reach - early) * block, points), BF16),
        ],
        in_specs=[hbm] * 6,
        out_specs=[vmem] * (2 * ways + 1),
        scratch_shapes=[
            pltpu.VMEM((functions + 1, 16, LANES), F32),
            pltpu.VMEM((height, LANES), F32),
            pltpu.SMEM((atoms,), jnp.int32),
            pltpu.VMEM((depth, block, points), BF16),
            pltpu.VMEM((functions, functions, pairs), F32),
            pltpu.VMEM((1, pairs), jnp.int32),
            pltpu.VMEM((1, pairs), jnp.int32),
            pltpu.VMEM((1, pairs), jnp.int32),
            pltpu.SemaphoreType.DMA((functions,)),
            pltpu.SemaphoreType.DMA((6,)),
        ],
        compiler_params=pltpu.CompilerParams(vmem_limit_bytes=8 << 20),
        name="pack",
    )(
        fixed(anchor),
        fixed(support.transpose(1, 2, 0, 3)),
        fixed(kernel.transpose(1, 2, 0)),
        fixed(pair_owner.reshape(1, pairs)),
        fixed(pair_partner.reshape(1, pairs)),
        fixed(pair_live.reshape(1, pairs)),
    )
    own, onward, tail = packed[:ways], packed[ways : 2 * ways], packed[2 * ways]
    upper, peers = [], []
    for k in range(ways):
        upper.append(moved_by(onward[k], ("space", "orb"), (1, k)))
    for k in range(1, ways):
        peers.append(moved_by(own[k], ("orb",), (k,)))
    tail = moved_by(tail, ("space", "orb"), (1, ways - 1))
    sources = [own[0]] + peers + upper

    rows = functions * band
    size = spans_of(functions, pairs, band)[1]
    head = round_up(groups * functions, 8)
    order = [0] + [ways] + list(range(1, ways)) + [ways + k for k in range(1, ways)]
    kept = [
        pltpu.VMEM((rows, planes * points), BF16),
        pltpu.VMEM((rows, round_up(2 * rows, LANES)), BF16),
        pltpu.VMEM((2 * ways, *size), BF16),
        pltpu.VMEM((2 * ways, atoms, LANES), F32),
    ]
    held = pl.pallas_call(
        functools.partial(first_kernel, dims),
        out_shape=kept,
        in_specs=[vmem],
        out_specs=[vmem] * 4,
        compiler_params=pltpu.CompilerParams(vmem_limit_bytes=8 << 20),
        name="first",
    )(sources[0])
    for c in order[1:]:
        held = pl.pallas_call(
            functools.partial(next_kernel, dims, c),
            out_shape=kept,
            in_specs=[vmem] + [vmem] * 4,
            out_specs=[vmem] * 4,
            input_output_aliases={1 + i: i for i in range(4)},
            compiler_params=pltpu.CompilerParams(vmem_limit_bytes=8 << 20),
        )(sources[c], *held)
    f_all, d_all, tables, owns = held
    parts = pl.pallas_call(
        functools.partial(main_kernel, dims, order[-1]),
        out_shape=[jax.ShapeDtypeStruct((head + round_up(planes, 8), LANES), F32)] * ways
        + [jax.ShapeDtypeStruct((head, LANES), F32)] * ways
        + kept[:1],
        in_specs=[vmem] * 6,
        out_specs=[vmem] * (2 * ways + 1),
        scratch_shapes=[pltpu.VMEM((rows, planes * points), BF16)],
        input_output_aliases={5: 2 * ways},
        compiler_params=pltpu.CompilerParams(vmem_limit_bytes=20 << 20),
        name="main",
    )(v_ext, tail, d_all, tables, owns, f_all)
    parts = parts[: 2 * ways]

    own_parts, low_parts = parts[:ways], parts[ways:]
    messages, arrived = [own_parts[0]], []
    for k in range(ways):
        arrived.append(moved_by(low_parts[k], ("space", "orb"), (-1, -k)))
    for k in range(1, ways):
        messages.append(moved_by(own_parts[k], ("orb",), (-k,)))
    mine = arrived[0]
    for part in arrived[1:]:
        mine = mine + part
    for message in messages:
        mine = mine + message[:head]
    shares = lax.axis_size("grid")
    other = moved_by(mine, ("grid",), (1,))
    for k in range(2, shares):
        other = other + moved_by(mine, ("grid",), (k,))
    density, blocks = pl.pallas_call(
        functools.partial(final_kernel, dims),
        out_shape=[
            jax.ShapeDtypeStruct((slab, points), F32),
            jax.ShapeDtypeStruct((functions, functions, pairs), F32),
        ],
        in_specs=[vmem] * (2 + ways),
        out_specs=[hbm] * 2,
        scratch_shapes=[
            pltpu.VMEM((slab, points), F32),
            pltpu.VMEM((functions, functions, pairs), F32),
            pltpu.VMEM((functions, functions, LANES), F32),
            pltpu.SemaphoreType.DMA((2,)),
        ],
        compiler_params=pltpu.CompilerParams(vmem_limit_bytes=4 << 20),
        name="final",
    )(mine, other, *messages)
    return (density, blocks.transpose(2, 0, 1))


def solution(mesh):
    placed = (
        P(("shift", "space", "orb"), None, None, "grid"),
        P(("shift", "space", "orb")),
        P(("shift", "space", "orb"), None, None),
        P(("shift", "space", "orb")),
        P(("shift", "space", "orb")),
        P(("shift", "space", "orb")),
        P(("shift", "space"), "grid"),
    )
    return jax.shard_map(
        on_device,
        mesh=mesh,
        in_specs=placed,
        out_specs=(P(("shift", "space"), "grid"), P(("shift", "space", "orb"), None, None)),
        check_vma=False,
    )
```
